32 devices in a mesh: aux: 4 (over x, core), orb: 8 (over z, y).
Axes of the slice: x: 2, y: 2, z: 4, core: 2. Of those that a mesh axis runs over, the one named last changes fastest.
Arguments:
- three_center: bfloat16 [640, 8, 3, 4096], P(('aux', 'orb')), may hold values from -1.5 to 1.5
- atom_size: int32 [8], replicated, may hold values from 32 to 64
- tensor_pattern: int32 [40, 8, 3], P('aux', 'orb'), may hold values 0 or 1
- green_occ: bfloat16 [8, 3, 4096], P('orb'), may hold values from -0.5 to 0.5
- green_virt: bfloat16 [8, 3, 4096], P('orb'), may hold values from -0.5 to 0.5
- green_pattern: int32 [8, 3], P('orb'), may hold values 0 or 1
Outputs:
- chi: float32 [640, 640], P(('aux', 'orb'))
The draws below stay inside these ranges and needn't reach their ends.
Inputs may be any that keep to these rules, and one draw needn't show every extreme that they name: `atom_size`: functions in use per block.
All inputs are finite; a program needn't handle non-finite values. No bound on the sum of `tensor_pattern` or of `green_pattern` on one device may be relied on, other than what follows from the above.
Results may differ from the reference program's by a relative error of at most 0.0041.
Values may be sent and summed in bfloat16 or wider, within the bound.
A program may use at most 128 MiB of HBM per device.

```python
import jax
import jax.numpy as jnp
from jax import lax

BS = 64
R = 1
W = 3
ABS = 16
AUX_DEV = 160
NAUX = 640
NOB = 8
NAB = 40
N_AUX = 4


def set_ends(drawn, key, low, largest):
    dims = drawn.shape
    spot = [jax.random.randint(jax.random.fold_in(key, axis), (), 0, dims[axis]) for axis in range(len(dims))]
    drawn = drawn.at[tuple(spot)].set(low)
    longest = dims.index(max(dims))
    spot[longest] = (spot[longest] + 1) % dims[longest]
    return drawn.at[tuple(spot)].set(largest)


def strengthened(entries, key, source, target, shards_of, factor):
    owner, partner = [(jnp.arange(entries.shape[position]) // (entries.shape[position] // shards_of)).reshape([-1 if axis == position else 1 for axis in range(entries.ndim)]) for position in (source, target)]
    chosen = jax.random.permutation(key, shards_of)[partner]
    strong = (owner == chosen) | (owner == (partner + shards_of // 2) % shards_of)
    return jnp.where(strong, factor * entries, entries)


def block_levels(key, shape, split, least, largest):
    level, own = 1.0, jax.random.fold_in(key, 6)
    for axis_at, parts in split:
        steps = jnp.exp(jax.random.uniform(jax.random.fold_in(own, axis_at), (parts,), jnp.float32, least / len(split), largest / len(split)))
        level = level * jnp.repeat(steps, shape[axis_at] // parts).reshape([-1 if axis == axis_at else 1 for axis in range(len(shape))])
    return level


def gaussian(key, extent, width, most, pieces=(), kind=jnp.bfloat16):
    values = jax.random.normal(key, extent, jnp.float32) * width
    if len(pieces) > 0:
        values = block_levels(key, extent, pieces, -0.22, 0.18) * values
    return jnp.clip(values, min=-most, max=most).astype(kind)


def bell_draw_with(stream_key, shape, spread, limit, split, heavy, kind=jnp.bfloat16):
    drawn = spread * jax.random.normal(stream_key, shape, jnp.float32)
    if split:
        drawn = drawn * block_levels(stream_key, shape, split, -0.22, 0.18)
    return jnp.clip(strengthened(drawn, jax.random.fold_in(stream_key, 3), *heavy), -limit, limit).astype(kind)


def setup_inputs(seed: int = 0) -> dict:
    splits = jax.random.split(jax.random.key(seed), 7)
    three_center = bell_draw_with(splits[0], (NAUX, NOB, W, BS * BS), ((NOB * BS * BS) ** -0.25), 1.5, ((0, 32),), (1, 0, 8, 2.0))
    atom_size = set_ends(jax.random.randint(splits[1], (NOB,), BS // 2, BS + 1), jax.random.fold_in(splits[1], 1), BS // 2, BS).astype(jnp.int32)
    tensor_pattern = set_ends((jax.random.randint(splits[2], (NAB, NOB, W), 0, 4) < 3).astype(jnp.int32), jax.random.fold_in(splits[2], 1), 0, 1)
    green_occ = gaussian(splits[3], (NOB, W, BS * BS), (2 * BS) ** -0.5, 0.5, ((0, 8),))
    green_virt = gaussian(splits[4], (NOB, W, BS * BS), (2 * BS) ** -0.5, 0.5, ((0, 8),))
    green_pattern = set_ends((jax.random.randint(splits[5], (NOB, W), 0, 4) < 3).astype(jnp.int32), jax.random.fold_in(splits[5], 1), 0, 1)
    return dict(three_center=three_center, atom_size=atom_size, tensor_pattern=tensor_pattern, green_occ=green_occ, green_virt=green_virt, green_pattern=green_pattern)


def block_masks(atom_size, first_block, local_blocks):
    total_blocks = atom_size.shape[0]
    owned = first_block + jnp.arange(local_blocks, dtype=jnp.int32)
    offsets = jnp.arange(W, dtype=jnp.int32)
    partner = owned[:, None] + offsets[None, :] - R
    inside = (partner >= 0) & (partner < total_blocks)
    catalog = jnp.arange(total_blocks, dtype=jnp.int32)
    size_partner = jnp.sum(jnp.where(partner[:, :, None] == catalog, atom_size, 0), axis=2)
    size_owned = jnp.sum(jnp.where(owned[:, None] == catalog, atom_size, 0), axis=1)
    funcs = jnp.arange(BS, dtype=jnp.int32)
    rows_ok = (funcs[None, None, :] < size_partner[:, :, None]) & inside[:, :, None]
    cols_ok = funcs[None, :] < size_owned[:, None]
    pair_ok = rows_ok[:, :, :, None] & cols_ok[:, None, None, :]
    return inside, pair_ok.reshape(local_blocks, W, BS * BS)


def first_products(padded_occ, tensor):
    rows = tensor.shape[0]
    local_blocks = tensor.shape[1]
    results = []
    for target in range(W):
        total = jnp.zeros((rows, local_blocks, BS, BS), jnp.float32)
        for source in range(W):
            if abs(target - source) <= R:
                green = padded_occ[source:source + local_blocks, target - source + R].reshape(local_blocks, BS, BS)
                block = tensor[:, :, source].reshape(rows, local_blocks, BS, BS)
                total = total + jnp.einsum("nlm,pnmv->pnlv", green.astype(jnp.float32), block.astype(jnp.float32))
        results.append(total.reshape(rows, local_blocks, BS * BS))
    return jnp.stack(results, axis=2).astype(jnp.bfloat16)


def second_products(padded_tensor, virt):
    rows = padded_tensor.shape[0]
    local_blocks = virt.shape[0]
    results = []
    for target in range(W):
        total = jnp.zeros((rows, local_blocks, BS, BS), jnp.float32)
        for source in range(W):
            if abs(target - source) <= R:
                block = padded_tensor[:, source:source + local_blocks, target - source + R].reshape(rows, local_blocks, BS, BS)
                green = virt[:, source].reshape(local_blocks, BS, BS)
                total = total + jnp.einsum("pnls,nsv->pnlv", block.astype(jnp.float32), green.astype(jnp.float32))
        results.append(total.reshape(rows, local_blocks, BS * BS))
    return jnp.stack(results, axis=2).astype(jnp.bfloat16)


def reference(three_center, atom_size, tensor_pattern, green_occ, green_virt, green_pattern):
    inside, pair_ok = block_masks(atom_size, jnp.int32(0), NOB)
    pattern_rows = jnp.repeat(tensor_pattern, ABS, axis=0)
    keep = (pattern_rows[..., None] > 0) & pair_ok[None]
    tensor = jnp.where(keep, three_center, jnp.zeros((), three_center.dtype))
    diagonal = jnp.arange(W, dtype=jnp.int32) == R
    green_keep = ((green_pattern > 0) | diagonal[None, :]) & inside
    green_mask = green_keep[..., None] & pair_ok
    occ = jnp.where(green_mask, green_occ, jnp.zeros((), green_occ.dtype))
    virt = jnp.where(green_mask, green_virt, jnp.zeros((), green_virt.dtype))
    padded_occ = jnp.pad(occ, ((R, R), (0, 0), (0, 0)))
    groups = tensor.reshape(N_AUX, AUX_DEV, NOB, W, BS * BS)

    def second_group(group):
        return second_products(jnp.pad(group, ((0, 0), (R, R), (0, 0), (0, 0))), virt)

    second = lax.map(second_group, groups).reshape(NAUX, NOB * W * BS * BS)

    def chi_group(group):
        first = first_products(padded_occ, group).reshape(AUX_DEV, NOB * W * BS * BS)
        return lax.dot_general(first, second, (((1,), (1,)), ((), ())), preferred_element_type=jnp.float32)

    return lax.map(chi_group, groups).reshape(NAUX, NAUX)
```

```python
import functools

import jax
import jax.numpy as jnp
from jax import lax
from jax.experimental import pallas as pl
from jax.experimental.pallas import tpu as pltpu
from jax.sharding import PartitionSpec as P

BS = 64
R = 1
W = 3
ABS = 16
LANES = 128
SUB = 8
TILES = BS * BS // LANES
PER = LANES // BS


def unit_shape(rows):
    rest = rows % SUB
    tiles = SUB // rest if rest else 1
    return tiles, (rows // SUB) * tiles + (1 if rest else 0)


def gather(x, axis):
    count = 1
    for name in axis if isinstance(axis, tuple) else (axis,):
        count *= lax.axis_size(name)
    return lax.all_to_all(
        jnp.broadcast_to(x[None], (count,) + x.shape), axis, split_axis=0, concat_axis=0, tiled=True
    )


def write_unit(out_ref, unit, rows, load):
    tiles, pieces = unit_shape(rows)
    whole = rows // SUB
    rest = rows % SUB
    for j in range(tiles):
        for q in range(whole):
            out_ref[unit * pieces + j * whole + q] = load(j, q * SUB).astype(out_ref.dtype)
    if rest:
        place = lax.broadcasted_iota(jnp.int32, (SUB, LANES), 0) // rest
        last = load(0, whole * SUB)
        for j in range(1, tiles):
            last = jnp.where(place == j, load(j, whole * SUB - j * rest), last)
        out_ref[unit * pieces + tiles * whole] = last.astype(out_ref.dtype)


def clear_tail(out_ref, begin, rows):
    _, pieces = unit_shape(rows)
    none = jnp.zeros((SUB, LANES), out_ref.dtype)

    def clear(i, carry):
        out_ref[i] = none
        return carry

    lax.fori_loop(begin * pieces, out_ref.shape[0], clear, 0)


def send_kernel(offset_ref, t_ref, out_ref, wide_ref):
    rows, _, blocks, _ = t_ref.shape
    tiles, _ = unit_shape(rows)
    step = W * TILES * blocks

    def widen(p, carry):
        for d in range(W):
            x = t_ref[p, d].astype(jnp.float32)
            for i in range(TILES):
                at = pl.multiple_of(p * step + (d * TILES + i) * blocks, SUB)
                wide_ref[pl.ds(at, blocks), :] = x[:, i * LANES : (i + 1) * LANES]
        return carry

    lax.fori_loop(0, rows, widen, 0)

    def block(b, carry):
        n, d = b // W, b % W
        first = offset_ref[b]

        def unit(u, c):
            def load(j, p):
                at = p * step + (d * TILES + u * tiles + j) * blocks + n
                return wide_ref[pl.ds(at, SUB, stride=step), :]

            write_unit(out_ref, first + u, rows, load)
            return c

        lax.fori_loop(0, offset_ref[b + 1] - first, unit, 0)
        return carry

    lax.fori_loop(0, blocks * W, block, 0)
    clear_tail(out_ref, offset_ref[blocks * W], rows)


def send_layout(three_center, offsets, units):
    rows, blocks = three_center.shape[:2]
    _, pieces = unit_shape(rows)
    reach = rows // SUB * SUB + SUB
    return pl.pallas_call(
        send_kernel,
        in_specs=[
            pl.BlockSpec(memory_space=pltpu.SMEM),
            pl.BlockSpec(memory_space=pltpu.VMEM),
        ],
        out_specs=pl.BlockSpec(memory_space=pltpu.VMEM),
        out_shape=jax.ShapeDtypeStruct((units * pieces, SUB, LANES), jnp.bfloat16),
        scratch_shapes=[pltpu.VMEM((reach * W * TILES * blocks, LANES), jnp.float32)],
        compiler_params=pltpu.CompilerParams(vmem_limit_bytes=48 << 20),
        cost_estimate=pl.CostEstimate(
            flops=0, bytes_accessed=three_center.size * 16, transcendentals=0
        ),
    )(offsets, three_center.transpose(0, 2, 1, 3))


def x_kernel(offset_ref, keep_ref, t_ref, v_ref, o_ref, out_ref, wide_ref, t2_ref, second_ref, x_ref):
    rows, _, blocks, _ = t_ref.shape
    tiles, _ = unit_shape(rows)
    depth = W * TILES

    def turn(p, carry):
        for d in range(W):
            x = t_ref[p, d].astype(jnp.float32)
            for i in range(TILES):
                wide_ref[i * blocks : (i + 1) * blocks, :] = x[:, i * LANES : (i + 1) * LANES]
            for n in range(blocks):
                kept = wide_ref[pl.ds(n, TILES, stride=blocks), :] * keep_ref[p, n * W + d]
                at = pl.multiple_of(p * TILES, TILES)
                t2_ref[n * W + d, pl.ds(at, TILES), :] = kept.astype(t2_ref.dtype)
        return carry

    lax.fori_loop(0, rows, turn, 0)
    lane = lax.broadcasted_iota(jnp.int32, (1, LANES), 1)

    def block(n, carry):
        for e in range(W):
            total = None
            for d in range(W):
                if abs(e - d) <= R:
                    m = jnp.clip(n + d - R, 0, blocks - 1)
                    part = jnp.dot(
                        t2_ref[m * W + e - d + R], v_ref[n * W + d], preferred_element_type=jnp.float32
                    )
                    total = part if total is None else total + part
            total = total.astype(second_ref.dtype)
            for p in range(rows):
                for h in range(PER):
                    at = h * depth + e * TILES
                    second_ref[at : at + TILES, p * LANES : (p + 1) * LANES] = total[
                        p * TILES : (p + 1) * TILES, h * LANES : (h + 1) * LANES
                    ]
        chunk = 5 if rows % 5 == 0 else 1
        for c in range(rows // chunk):
            both = jnp.dot(
                o_ref[n],
                second_ref[:, c * chunk * LANES : (c + 1) * chunk * LANES],
                preferred_element_type=jnp.float32,
            )
            for i in range(chunk):
                p = c * chunk + i
                at = slice(i * LANES, (i + 1) * LANES)
                x_ref[p * depth : (p + 1) * depth, :] = jnp.where(
                    lane < BS, both[:depth, at], both[depth:, at]
                )
        for d in range(W):
            first = offset_ref[n * W + d]

            def unit(u, c):
                def load(j, p):
                    at = p * depth + d * TILES + u * tiles + j
                    return x_ref[pl.ds(at, SUB, stride=depth), :]

                write_unit(out_ref, first + u, rows, load)
                return c

            lax.fori_loop(0, offset_ref[n * W + d + 1] - first, unit, 0)
        return carry

    lax.fori_loop(0, blocks, block, 0)
    clear_tail(out_ref, offset_ref[blocks * W], rows)


def x_layout(three_center, offsets, keep, virt4, occ2, units):
    rows, blocks = three_center.shape[:2]
    _, pieces = unit_shape(rows)
    depth = W * TILES
    reach = rows // SUB * SUB + SUB
    return pl.pallas_call(
        x_kernel,
        in_specs=[pl.BlockSpec(memory_space=pltpu.SMEM)] * 2
        + [pl.BlockSpec(memory_space=pltpu.VMEM)] * 3,
        out_specs=pl.BlockSpec(memory_space=pltpu.VMEM),
        out_shape=jax.ShapeDtypeStruct((units * pieces, SUB, LANES), jnp.bfloat16),
        scratch_shapes=[
            pltpu.VMEM((TILES * blocks, LANES), jnp.float32),
            pltpu.VMEM((blocks * W, rows * TILES, LANES), jnp.bfloat16),
            pltpu.VMEM((PER * depth, rows * LANES), jnp.bfloat16),
            pltpu.VMEM((reach * depth, LANES), jnp.float32),
        ],
        compiler_params=pltpu.CompilerParams(vmem_limit_bytes=48 << 20),
        cost_estimate=pl.CostEstimate(
            flops=blocks * rows * (7 * TILES * LANES * LANES * 4 + 16 * TILES * TILES * 9 * LANES),
            bytes_accessed=three_center.size * 8,
            transcendentals=0,
        ),
    )(offsets, keep, three_center.transpose(0, 2, 1, 3), virt4, occ2)


def chi_kernel(rows, left_ref, right_ref, keep_ref, out_ref, l_ref, r_ref):
    sources = left_ref.shape[0]
    tiles, pieces = unit_shape(rows)
    units = left_ref.shape[1] // pieces
    whole, rest = rows // SUB, rows % SUB
    main = sources * whole * SUB

    def assemble(from_ref, to_ref):
        for u in range(units):
            for j in range(tiles):
                at = slice((u * tiles + j) * LANES, (u * tiles + j + 1) * LANES)
                for s in range(sources):
                    if whole:
                        i = u * pieces + j * whole
                        to_ref[s * whole * SUB : (s + 1) * whole * SUB, at] = jnp.concatenate(
                            [from_ref[s, i + q] for q in range(whole)], axis=0
                        )
                if rest:
                    i = u * pieces + tiles * whole
                    for s in range(0, sources, tiles):
                        to_ref[main + s * rest : main + (s + tiles) * rest, at] = jnp.concatenate(
                            [from_ref[s + t, i, j * rest : (j + 1) * rest, :] for t in range(tiles)],
                            axis=0,
                        )

    assemble(left_ref, l_ref)
    for i in range(units * tiles):
        at = slice(i * LANES, (i + 1) * LANES)
        l_ref[:, at] = l_ref[:, at] * keep_ref[:, i : i + 1]
    assemble(right_ref, r_ref)
    chi = lax.dot_general(
        l_ref[...], r_ref[...], (((1,), (1,)), ((), ())), preferred_element_type=jnp.float32
    ).astype(out_ref.dtype)
    groups, height = out_ref.shape[:2]
    top = main // groups
    for a in range(groups):
        out_ref[a, :top, :] = chi[a * top : (a + 1) * top]
        if rest:
            low = height - top
            out_ref[a, top:, :] = chi[main + a * low : main + (a + 1) * low]


def chi_part(left, right, keep, rows, groups):
    sources = left.shape[0]
    tiles, pieces = unit_shape(rows)
    functions = sources * rows
    depth = left.shape[1] // pieces * tiles * LANES
    return pl.pallas_call(
        functools.partial(chi_kernel, rows),
        in_specs=[pl.BlockSpec(memory_space=pltpu.VMEM)] * 3,
        out_specs=pl.BlockSpec(memory_space=pltpu.VMEM),
        out_shape=jax.ShapeDtypeStruct((groups, functions // groups, functions), jnp.bfloat16),
        scratch_shapes=[pltpu.VMEM((functions, depth), jnp.bfloat16)] * 2,
        compiler_params=pltpu.CompilerParams(vmem_limit_bytes=56 << 20),
    )(left, right, keep)


def pair_masks(atom_size, blocks):
    owned = jnp.arange(blocks, dtype=jnp.int32)[:, None]
    partner = owned + jnp.arange(W, dtype=jnp.int32)[None, :] - R
    inside = (partner >= 0) & (partner < blocks)
    catalog = jnp.arange(blocks, dtype=jnp.int32)
    partner_size = jnp.sum(jnp.where(partner[:, :, None] == catalog, atom_size, 0), axis=2)
    funcs = jnp.arange(BS, dtype=jnp.int32)
    rows_ok = (funcs[None, None, :] < partner_size[:, :, None]) & inside[:, :, None]
    cols_ok = funcs[None, :] < atom_size[:, None]
    return inside, partner_size, rows_ok[:, :, :, None] & cols_ok[:, None, None, :]


def green_operands(occ, virt):
    blocks = occ.shape[0]
    zero = jnp.zeros_like(virt)
    virt4 = jnp.concatenate(
        [
            jnp.concatenate([virt, zero, zero, virt], axis=3),
            jnp.concatenate([zero, virt, virt, zero], axis=3),
        ],
        axis=2,
    ).reshape(blocks * W, PER * BS, PER * PER * BS)
    half = jnp.arange(BS, dtype=jnp.int32)
    order = (half % TILES) * PER + half // TILES
    pick = (order[:, None] == half[None, :]).astype(occ.dtype)
    split = jnp.einsum("ndlm,jm,il->ndji", occ, pick, pick, preferred_element_type=jnp.float32)
    split = split.astype(occ.dtype).reshape(blocks, W, PER, TILES, PER, TILES)
    padded = jnp.pad(split, ((R, R),) + ((0, 0),) * 5)
    none = jnp.zeros((blocks, TILES, TILES), occ.dtype)
    lines = []
    for p in range(PER):
        for d in range(W):
            parts = []
            for h in range(PER):
                for e in range(W):
                    if abs(e - d) <= R:
                        parts.append(padded[d : d + blocks, e - d + R, p, :, (p + h) % PER, :])
                    else:
                        parts.append(none)
            lines.append(jnp.concatenate(parts, axis=2))
    return virt4, jnp.concatenate(lines, axis=1)


def shared(share, offsets, three_center, atom_size, tensor_pattern, green_occ, green_virt, green_pattern):
    both = ("aux", "orb")
    n_aux, n_orb = lax.axis_size("aux"), lax.axis_size("orb")
    aux, orb = lax.axis_index("aux"), lax.axis_index("orb")
    rows, blocks = three_center.shape[0], three_center.shape[1]
    local_blocks = green_occ.shape[0]
    area = BS * BS
    targets = n_aux * n_orb
    functions = targets * rows
    tiles, pieces = unit_shape(rows)

    inside, _, pair_ok = pair_masks(atom_size, blocks)
    units = share * targets

    groups = tensor_pattern.shape[0]
    flags = jnp.concatenate([tensor_pattern.reshape(-1), green_pattern.reshape(-1)])
    flags = (flags > 0).astype(jnp.bfloat16)
    counts = (groups * local_blocks * W, local_blocks * W)
    lines = -(-flags.shape[0] // area)
    flags = jnp.pad(flags, (0, lines * area - flags.shape[0])).reshape(lines, area)
    packed = jnp.concatenate(
        [green_occ.reshape(-1, area), green_virt.reshape(-1, area), flags], axis=0
    )
    packed = gather(packed, "orb")

    outgoing = send_layout(three_center, offsets, units)
    left = lax.all_to_all(
        outgoing.reshape(targets, share * pieces, SUB, LANES), both, split_axis=0, concat_axis=0, tiled=True
    )

    flags = packed[:, 2 * local_blocks * W :].reshape(n_orb, lines * area)
    pattern_orb = flags[:, : counts[0]].reshape(n_orb, groups, local_blocks, W)
    pattern_orb = pattern_orb.transpose(1, 0, 2, 3).reshape(groups, blocks * W)
    green_all = flags[:, counts[0] : counts[0] + counts[1]].reshape(blocks, W)
    keep = jnp.repeat(pattern_orb, ABS, axis=0)
    keep = lax.dynamic_slice_in_dim(keep, orb * rows, rows, axis=0).astype(jnp.float32)

    diagonal = jnp.arange(W, dtype=jnp.int32) == R
    green_keep = ((green_all > 0) | diagonal[None, :]) & inside
    green_mask = green_keep[..., None, None] & pair_ok
    half = local_blocks * W
    occ = packed[:, :half].reshape(blocks, W, BS, BS)
    virt = packed[:, half : 2 * half].reshape(blocks, W, BS, BS)
    occ = jnp.where(green_mask, occ, jnp.zeros((), occ.dtype))
    virt = jnp.where(green_mask, virt, jnp.zeros((), virt.dtype))
    virt4, occ2 = green_operands(occ, virt)

    x = x_layout(three_center, offsets, keep, virt4, occ2, units)
    right = lax.all_to_all(
        x.reshape(targets, share * pieces, SUB, LANES), both, split_axis=0, concat_axis=0, tiled=True
    )

    pattern = gather(pattern_orb, "aux").reshape(n_aux * groups, blocks * W)
    me = aux * n_orb + orb
    mine = (me * share + jnp.arange(share * tiles, dtype=jnp.int32) // tiles)[None, :]
    held = (mine >= offsets[:-1, None]) & (mine < offsets[1:, None])
    kept = jnp.dot(pattern, held.astype(jnp.bfloat16), preferred_element_type=jnp.float32)
    kept = jnp.repeat(kept.astype(jnp.bfloat16), ABS, axis=0).reshape(targets, rows, share * tiles)
    whole = rows // SUB * SUB
    kept = jnp.concatenate(
        [
            kept[:, :whole].reshape(targets * whole, share * tiles),
            kept[:, whole:].reshape(targets * (rows - whole), share * tiles),
        ],
        axis=0,
    )

    part = chi_part(left, right, kept, rows, n_aux)
    part = lax.all_to_all(part, "aux", split_axis=0, concat_axis=0, tiled=True)
    part = jnp.sum(part.astype(jnp.float32), axis=0).astype(jnp.bfloat16)
    part = jnp.concatenate(
        [
            part[: n_orb * whole].reshape(n_orb, whole, functions),
            part[n_orb * whole :].reshape(n_orb, rows - whole, functions),
        ],
        axis=1,
    )
    part = lax.all_to_all(part, "orb", split_axis=0, concat_axis=0, tiled=True)
    chi = jnp.sum(part.astype(jnp.float32), axis=0)
    chi = jnp.concatenate(
        [
            chi[:, : targets * whole].reshape(rows, targets, whole),
            chi[:, targets * whole :].reshape(rows, targets, rows - whole),
        ],
        axis=2,
    )
    return chi.reshape(rows, functions)


def body(three_center, atom_size, *others):
    targets = lax.axis_size("aux") * lax.axis_size("orb")
    blocks = three_center.shape[1]
    tiles, _ = unit_shape(three_center.shape[0])
    inside, partner_size, _ = pair_masks(atom_size, blocks)
    taken = -(-partner_size // (PER * tiles)) * inside
    before = jnp.arange(blocks * W + 1, dtype=jnp.int32)[:, None]
    before = before > jnp.arange(blocks * W, dtype=jnp.int32)[None, :]
    offsets = jnp.sum(jnp.where(before, taken.reshape(1, -1), 0), axis=1).astype(jnp.int32)
    largest = -(-(blocks * W - 2 * R) * TILES // (tiles * targets))
    least = -(-largest // 2)
    needed = -(-offsets[-1] // targets)
    return lax.switch(
        jnp.clip(needed, least, largest) - least,
        [functools.partial(shared, share) for share in range(least, largest + 1)],
        offsets,
        three_center,
        atom_size,
        *others,
    )


def solution(mesh):
    return jax.shard_map(
        body,
        mesh=mesh,
        in_specs=(
            P(("aux", "orb"), None, None, None),
            P(),
            P("aux", "orb", None),
            P("orb", None, None),
            P("orb", None, None),
            P("orb", None),
        ),
        out_specs=P(("aux", "orb"), None),
        check_vma=False,
    )
```

```python
import functools

import jax
import jax.numpy as jnp
from jax import lax
from jax.experimental import pallas as pl
from jax.experimental.pallas import tpu as pltpu
from jax.sharding import PartitionSpec as P

BS = 64
R = 1
W = 3
ABS = 16
LANES = 128
SUB = 8
TILES = BS * BS // LANES
PER = LANES // BS


def unit_shape(rows):
    rest = rows % SUB
    tiles = SUB // rest if rest else 1
    return tiles, (rows // SUB) * tiles + (1 if rest else 0)


def gather(x, axis):
    count = 1
    for name in axis if isinstance(axis, tuple) else (axis,):
        count *= lax.axis_size(name)
    return lax.all_to_all(
        jnp.broadcast_to(x[None], (count,) + x.shape), axis, split_axis=0, concat_axis=0, tiled=True
    )


def write_unit(out_ref, unit, rows, load):
    tiles, pieces = unit_shape(rows)
    whole = rows // SUB
    rest = rows % SUB
    for j in range(tiles):
        for q in range(whole):
            out_ref[unit * pieces + j * whole + q] = load(j, q * SUB).astype(out_ref.dtype)
    if rest:
        place = lax.broadcasted_iota(jnp.int32, (SUB, LANES), 0) // rest
        last = load(0, whole * SUB)
        for j in range(1, tiles):
            last = jnp.where(place == j, load(j, whole * SUB - j * rest), last)
        out_ref[unit * pieces + tiles * whole] = last.astype(out_ref.dtype)


def clear_tail(out_ref, begin, rows):
    _, pieces = unit_shape(rows)
    none = jnp.zeros((SUB, LANES), out_ref.dtype)

    def clear(i, carry):
        out_ref[i] = none
        return carry

    lax.fori_loop(begin * pieces, out_ref.shape[0], clear, 0)


def send_kernel(offset_ref, t_ref, base_ref, more_ref, wide_ref):
    rows, _, blocks, _ = t_ref.shape
    tiles, pieces = unit_shape(rows)
    step = W * TILES * blocks
    split = base_ref.shape[0] // pieces

    def widen(p, carry):
        for d in range(W):
            x = t_ref[p, d].astype(jnp.float32)
            for i in range(TILES):
                at = pl.multiple_of(p * step + (d * TILES + i) * blocks, SUB)
                wide_ref[pl.ds(at, blocks), :] = x[:, i * LANES : (i + 1) * LANES]
        return carry

    lax.fori_loop(0, rows, widen, 0)

    def block(b, carry):
        n, d = b // W, b % W
        first = offset_ref[b]
        count = offset_ref[b + 1] - first
        turn = jnp.clip(split - first, 0, count)

        def unit(ref, begin, u, c):
            def load(j, p):
                at = p * step + (d * TILES + u * tiles + j) * blocks + n
                return wide_ref[pl.ds(at, SUB, stride=step), :]

            write_unit(ref, first + u - begin, rows, load)
            return c

        lax.fori_loop(0, turn, functools.partial(unit, base_ref, 0), 0)
        lax.fori_loop(turn, count, functools.partial(unit, more_ref, split), 0)
        return carry

    lax.fori_loop(0, blocks * W, block, 0)
    total = offset_ref[blocks * W]
    clear_tail(base_ref, jnp.minimum(total, split), rows)
    clear_tail(more_ref, jnp.maximum(total - split, 0), rows)


def send_layout(three_center, offsets, base_units, more_units):
    rows, blocks = three_center.shape[:2]
    _, pieces = unit_shape(rows)
    reach = rows // SUB * SUB + SUB
    return pl.pallas_call(
        send_kernel,
        in_specs=[
            pl.BlockSpec(memory_space=pltpu.SMEM),
            pl.BlockSpec(memory_space=pltpu.VMEM),
        ],
        out_specs=[pl.BlockSpec(memory_space=pltpu.VMEM)] * 2,
        out_shape=[
            jax.ShapeDtypeStruct((units * pieces, SUB, LANES), jnp.bfloat16)
            for units in (base_units, more_units)
        ],
        scratch_shapes=[pltpu.VMEM((reach * W * TILES * blocks, LANES), jnp.float32)],
        compiler_params=pltpu.CompilerParams(vmem_limit_bytes=48 << 20),
        cost_estimate=pl.CostEstimate(
            flops=0, bytes_accessed=three_center.size * 16, transcendentals=0
        ),
    )(offsets, three_center.transpose(0, 2, 1, 3))


def green_factors(limit_ref, green_ref, blocks, gm_ref, z_ref, v_ref, o_ref):
    local = blocks // green_ref.shape[0]
    row = lax.broadcasted_iota(jnp.int32, (BS, LANES), 0)
    lane = lax.broadcasted_iota(jnp.int32, (BS, LANES), 1)
    for b in range(blocks * W):
        n, d = b // W, b % W
        at = (n % local * W + d) * BS
        g = green_ref[n // local, at : at + BS, :].astype(jnp.float32)
        g = jnp.where((row < limit_ref[2 * b]) & (lane % BS < limit_ref[2 * b + 1]), g, 0.0)
        gm_ref[b * BS : (b + 1) * BS, :] = g.astype(gm_ref.dtype)
        left = jnp.where(lane < BS, pltpu.roll(g, BS, 1), 0.0).astype(v_ref.dtype)
        right = jnp.where(lane >= BS, g, 0.0).astype(v_ref.dtype)
        v_ref[b, :BS, :LANES] = left
        v_ref[b, :BS, LANES:] = right
        v_ref[b, BS:, :LANES] = right
        v_ref[b, BS:, LANES:] = left
    pick = (lane == row % TILES * PER + row // TILES).astype(gm_ref.dtype)
    turned = lax.dot_general(
        pick, gm_ref[...], (((1,), (1,)), ((), ())), preferred_element_type=jnp.float32
    ).astype(gm_ref.dtype)
    pairs = blocks * W // PER
    stacked = jnp.concatenate([turned[:, c * LANES : (c + 1) * LANES] for c in range(pairs)], axis=0)
    into = lax.broadcasted_iota(jnp.int32, (LANES, LANES), 1)
    source = into // BS * BS + into % TILES * PER + into % BS // TILES
    perm = (lax.broadcasted_iota(jnp.int32, (LANES, LANES), 0) == source).astype(gm_ref.dtype)
    z_ref[...] = jnp.dot(stacked, perm, preferred_element_type=jnp.float32).astype(z_ref.dtype)
    o_ref[...] = jnp.zeros(o_ref.shape, o_ref.dtype)
    for n in range(blocks):
        for p in range(PER):
            for d in range(W):
                m = n + d - R
                if m < 0 or m >= blocks:
                    continue
                to = (p * W + d) * TILES
                for h in range(PER):
                    for e in range(W):
                        if abs(e - d) <= R:
                            b = m * W + e - d + R
                            line = b // PER * BS + p * TILES
                            at = b % PER * BS + (p + h) % PER * TILES
                            col = (h * W + e) * TILES
                            o_ref[n, to : to + TILES, col : col + TILES] = z_ref[
                                line : line + TILES, at : at + TILES
                            ]


def x_kernel(
    offset_ref, keep_ref, limit_ref, t_ref, green_ref, out_ref,
    wide_ref, t2_ref, second_ref, x_ref, gm_ref, z_ref, v_ref, o_ref,
):
    rows, _, blocks, _ = t_ref.shape
    tiles, _ = unit_shape(rows)
    depth = W * TILES
    green_factors(limit_ref, green_ref, blocks, gm_ref, z_ref, v_ref, o_ref)

    def turn(p, carry):
        for d in range(W):
            x = t_ref[p, d].astype(jnp.float32)
            for i in range(TILES):
                wide_ref[i * blocks : (i + 1) * blocks, :] = x[:, i * LANES : (i + 1) * LANES]
            for n in range(blocks):
                kept = wide_ref[pl.ds(n, TILES, stride=blocks), :] * keep_ref[p, n * W + d]
                at = pl.multiple_of(p * TILES, TILES)
                t2_ref[n * W + d, pl.ds(at, TILES), :] = kept.astype(t2_ref.dtype)
        return carry

    lax.fori_loop(0, rows, turn, 0)
    lane = lax.broadcasted_iota(jnp.int32, (1, LANES), 1)

    def block(n, carry):
        for e in range(W):
            total = None
            for d in range(W):
                if abs(e - d) <= R:
                    m = jnp.clip(n + d - R, 0, blocks - 1)
                    part = jnp.dot(
                        t2_ref[m * W + e - d + R], v_ref[n * W + d], preferred_element_type=jnp.float32
                    )
                    total = part if total is None else total + part
            total = total.astype(second_ref.dtype)
            for p in range(rows):
                for h in range(PER):
                    at = h * depth + e * TILES
                    second_ref[at : at + TILES, p * LANES : (p + 1) * LANES] = total[
                        p * TILES : (p + 1) * TILES, h * LANES : (h + 1) * LANES
                    ]
        chunk = 5 if rows % 5 == 0 else 1
        for c in range(rows // chunk):
            both = jnp.dot(
                o_ref[n],
                second_ref[:, c * chunk * LANES : (c + 1) * chunk * LANES],
                preferred_element_type=jnp.float32,
            )
            for i in range(chunk):
                p = c * chunk + i
                at = slice(i * LANES, (i + 1) * LANES)
                x_ref[p * depth : (p + 1) * depth, :] = jnp.where(
                    lane < BS, both[:depth, at], both[depth:, at]
                )
        for d in range(W):
            first = offset_ref[n * W + d]

            def unit(u, c):
                def load(j, p):
                    at = p * depth + d * TILES + u * tiles + j
                    return x_ref[pl.ds(at, SUB, stride=depth), :]

                write_unit(out_ref, first + u, rows, load)
                return c

            lax.fori_loop(0, offset_ref[n * W + d + 1] - first, unit, 0)
        return carry

    lax.fori_loop(0, blocks, block, 0)
    clear_tail(out_ref, offset_ref[blocks * W], rows)


def x_layout(three_center, offsets, keep, limits, green, units):
    rows, blocks = three_center.shape[:2]
    _, pieces = unit_shape(rows)
    depth = W * TILES
    reach = rows // SUB * SUB + SUB
    return pl.pallas_call(
        x_kernel,
        in_specs=[pl.BlockSpec(memory_space=pltpu.SMEM)] * 3
        + [pl.BlockSpec(memory_space=pltpu.VMEM)] * 2,
        out_specs=pl.BlockSpec(memory_space=pltpu.VMEM),
        out_shape=jax.ShapeDtypeStruct((units * pieces, SUB, LANES), jnp.bfloat16),
        scratch_shapes=[
            pltpu.VMEM((TILES * blocks, LANES), jnp.float32),
            pltpu.VMEM((blocks * W, rows * TILES, LANES), jnp.bfloat16),
            pltpu.VMEM((PER * depth, rows * LANES), jnp.bfloat16),
            pltpu.VMEM((reach * depth, LANES), jnp.float32),
            pltpu.VMEM((blocks * W * BS, LANES), jnp.bfloat16),
            pltpu.VMEM((blocks * W // PER * BS, LANES), jnp.bfloat16),
            pltpu.VMEM((blocks * W, LANES, PER * LANES), jnp.bfloat16),
            pltpu.VMEM((blocks, PER * depth, PER * depth), jnp.bfloat16),
        ],
        compiler_params=pltpu.CompilerParams(vmem_limit_bytes=48 << 20),
        cost_estimate=pl.CostEstimate(
            flops=blocks * rows * (7 * TILES * LANES * LANES * 4 + 16 * TILES * TILES * 9 * LANES),
            bytes_accessed=three_center.size * 8,
            transcendentals=0,
        ),
    )(offsets, keep, limits, three_center.transpose(0, 2, 1, 3), green)


def exchange_kernel(base, more, most, more_ref, x_ref, keep_ref, out_ref, send_sem, recv_sem, own_sem):
    n_aux, n_orb = lax.axis_size("aux"), lax.axis_size("orb")
    targets = n_aux * n_orb
    aux, orb = lax.axis_index("aux"), lax.axis_index("orb")
    me = aux * n_orb + orb

    def spans(t, source):
        yield keep_ref, out_ref.at[source, pl.ds(2 * most + base, keep_ref.shape[0])]
        yield x_ref.at[pl.ds(t * base, base)], out_ref.at[source, pl.ds(most, base)]
        if more:
            at = pl.ds(targets * base + t * more, more)
            yield x_ref.at[at], out_ref.at[source, pl.ds(most + base, more)]
            yield more_ref.at[pl.ds(t * more, more)], out_ref.at[source, pl.ds(0, more)]

    def partner(i):
        return lax.rem(aux + lax.rem(i, n_aux), n_aux), lax.rem(orb + i // n_aux + n_orb // 2, n_orb)

    def copies(t, source, to):
        return [
            pltpu.make_async_remote_copy(
                src_ref=src,
                dst_ref=dst,
                send_sem=send_sem.at[k, t],
                recv_sem=recv_sem.at[k, source],
                device_id=to,
                device_id_type=pl.DeviceIdType.MESH,
            )
            for k, (src, dst) in enumerate(spans(t, source))
        ]

    def start(i, carry):
        to = partner(i)
        t = to[0] * n_orb + to[1]

        @pl.when(t != me)
        def _():
            for copy in copies(t, me, to):
                copy.start()

        return carry

    lax.fori_loop(0, targets, start, 0)
    own = [
        pltpu.make_async_copy(src, dst, own_sem.at[k]) for k, (src, dst) in enumerate(spans(me, me))
    ]
    for copy in own:
        copy.start()

    def finish(i, carry):
        to = partner(i)
        t = to[0] * n_orb + to[1]

        @pl.when(t != me)
        def _():
            for copy in copies(t, t, to):
                copy.wait_recv()
                copy.wait_send()

        return carry

    lax.fori_loop(0, targets, finish, 0)
    for copy in own:
        copy.wait()


def exchange(base, most, pieces, more, outgoing, x, keep):
    targets = lax.axis_size("aux") * lax.axis_size("orb")
    return pl.pallas_call(
        functools.partial(exchange_kernel, base * pieces, more * pieces, most * pieces),
        in_specs=[pl.BlockSpec(memory_space=pl.ANY)] * 3,
        out_specs=pl.BlockSpec(memory_space=pl.ANY),
        out_shape=jax.ShapeDtypeStruct(
            (targets, (2 * most + base) * pieces + keep.shape[0], SUB, LANES), jnp.bfloat16
        ),
        scratch_shapes=[
            pltpu.SemaphoreType.DMA((4, targets)),
            pltpu.SemaphoreType.DMA((4, targets)),
            pltpu.SemaphoreType.DMA((4,)),
        ],
        compiler_params=pltpu.CompilerParams(has_side_effects=True),
    )(outgoing, x, keep)


def chi_kernel(rows, share_ref, left_ref, both_ref, held_ref, out_ref, l_ref, r_ref, k_ref):
    sources = left_ref.shape[0]
    tiles, pieces = unit_shape(rows)
    base = left_ref.shape[1] // pieces
    most = (both_ref.shape[1] // pieces - base) // 2
    whole, rest = rows // SUB, rows % SUB
    main = sources * whole * SUB

    def assemble(from_ref, first, to_ref, u, tiles=tiles):
        for j in range(tiles):
            at = slice((u * tiles + j) * LANES, (u * tiles + j + 1) * LANES)
            for s in range(sources):
                if whole:
                    i = first + j * whole
                    to_ref[s * whole * SUB : (s + 1) * whole * SUB, at] = jnp.concatenate(
                        [from_ref[s, i + q] for q in range(whole)], axis=0
                    )
            if rest:
                i = first + tiles * whole
                step = SUB // rest
                for s in range(0, sources, step):
                    to_ref[main + s * rest : main + (s + step) * rest, at] = jnp.concatenate(
                        [from_ref[s + t, i, j * rest : (j + 1) * rest, :] for t in range(step)],
                        axis=0,
                    )

    assemble(both_ref, (2 * most + base) * pieces, k_ref, 0, 1)
    keep = jnp.dot(k_ref[...], held_ref[...], preferred_element_type=jnp.float32)
    keep = keep.astype(l_ref.dtype)

    def fill(u):
        if u < base:
            assemble(left_ref, u * pieces, l_ref, u)
        else:
            assemble(both_ref, (u - base) * pieces, l_ref, u)
        assemble(both_ref, (most + u) * pieces, r_ref, u)
        for i in range(u * tiles, (u + 1) * tiles):
            at = slice(i * LANES, (i + 1) * LANES)
            l_ref[:, at] = l_ref[:, at] * keep[:, i : i + 1]

    def clear(u):
        at = slice(u * tiles * LANES, (u + 1) * tiles * LANES)
        l_ref[:, at] = jnp.zeros((l_ref.shape[0], tiles * LANES), l_ref.dtype)
        r_ref[:, at] = jnp.zeros((r_ref.shape[0], tiles * LANES), r_ref.dtype)

    for u in range(base + most):
        if u < base:
            fill(u)
        else:
            pl.when(u < share_ref[0])(functools.partial(fill, u))
            pl.when(u >= share_ref[0])(functools.partial(clear, u))
    chi = lax.dot_general(
        l_ref[...], r_ref[...], (((1,), (1,)), ((), ())), preferred_element_type=jnp.float32
    ).astype(out_ref.dtype)
    groups, height = out_ref.shape[:2]
    top = main // groups
    for a in range(groups):
        out_ref[a, :top, :] = chi[a * top : (a + 1) * top]
        if rest:
            low = height - top
            out_ref[a, top:, :] = chi[main + a * low : main + (a + 1) * low]


def chi_part(share, left, both, held, rows, groups):
    sources = left.shape[0]
    tiles, pieces = unit_shape(rows)
    functions = sources * rows
    units = (left.shape[1] // pieces + both.shape[1] // pieces) // 2
    depth = units * tiles * LANES
    return pl.pallas_call(
        functools.partial(chi_kernel, rows),
        in_specs=[pl.BlockSpec(memory_space=pltpu.SMEM)]
        + [pl.BlockSpec(memory_space=pltpu.VMEM)] * 3,
        out_specs=pl.BlockSpec(memory_space=pltpu.VMEM),
        out_shape=jax.ShapeDtypeStruct((groups, functions // groups, functions), jnp.bfloat16),
        scratch_shapes=[pltpu.VMEM((functions, k), jnp.bfloat16) for k in (depth, depth, LANES)],
        compiler_params=pltpu.CompilerParams(vmem_limit_bytes=56 << 20),
    )(share, left, both, held)


def body(three_center, atom_size, tensor_pattern, green_occ, green_virt, green_pattern):
    both = ("aux", "orb")
    n_aux, n_orb = lax.axis_size("aux"), lax.axis_size("orb")
    aux, orb = lax.axis_index("aux"), lax.axis_index("orb")
    rows, blocks = three_center.shape[0], three_center.shape[1]
    local_blocks = green_occ.shape[0]
    area = BS * BS
    targets = n_aux * n_orb
    functions = targets * rows
    tiles, pieces = unit_shape(rows)

    owned = jnp.arange(blocks, dtype=jnp.int32)[:, None]
    partner = owned + jnp.arange(W, dtype=jnp.int32)[None, :] - R
    inside = (partner >= 0) & (partner < blocks)
    catalog = jnp.arange(blocks, dtype=jnp.int32)
    partner_size = jnp.sum(jnp.where(partner[:, :, None] == catalog, atom_size, 0), axis=2)
    taken = -(-partner_size // (PER * tiles)) * inside
    before = jnp.arange(blocks * W + 1, dtype=jnp.int32)[:, None]
    before = before > jnp.arange(blocks * W, dtype=jnp.int32)[None, :]
    offsets = jnp.sum(jnp.where(before, taken.reshape(1, -1), 0), axis=1).astype(jnp.int32)
    largest = -(-(blocks * W - 2 * R) * TILES // (tiles * targets))
    base = -(-largest // 2)
    most = largest - base
    more = jnp.clip(-(-offsets[-1] // targets) - base, 0, most)

    groups = tensor_pattern.shape[0]
    flags = [tensor_pattern.transpose(1, 2, 0).reshape(local_blocks * W, groups)]
    flags.append(green_pattern.reshape(local_blocks * W, 1))
    flags = (jnp.concatenate(flags, axis=1) > 0).astype(jnp.bfloat16)
    lines = -(-local_blocks * W // SUB) * SUB
    flags = jnp.pad(flags, ((0, lines - local_blocks * W), (0, LANES - groups - 1)))
    square = (local_blocks * W * BS, BS)
    packed = jnp.concatenate([green_occ.reshape(square), green_virt.reshape(square)], axis=1)
    packed = gather(jnp.concatenate([packed, flags], axis=0), "orb")

    first, outgoing = send_layout(three_center, offsets, base * targets, most * targets)
    packed, first = lax.optimization_barrier((packed, first))
    left = lax.all_to_all(
        first.reshape(targets, base * pieces, SUB, LANES), both, split_axis=0, concat_axis=0, tiled=True
    )

    flags = packed[:, square[0] : square[0] + local_blocks * W, :].reshape(blocks * W, LANES)
    mine = (orb * rows + jnp.arange(pieces * SUB, dtype=jnp.int32)) // ABS
    wanted = mine[:, None] == jnp.arange(LANES, dtype=jnp.int32)[None, :]
    keep = lax.dot_general(
        wanted.astype(flags.dtype),
        jnp.pad(flags, ((0, LANES - blocks * W), (0, 0))),
        (((1,), (1,)), ((), ())),
        preferred_element_type=jnp.float32,
    )
    held_pieces = rows // SUB + (1 if rows % SUB else 0)
    kept = keep[: held_pieces * SUB].astype(jnp.bfloat16).reshape(held_pieces, SUB, LANES)

    diagonal = jnp.arange(W, dtype=jnp.int32) == R
    green_all = flags[:, groups].reshape(blocks, W)
    green_keep = ((green_all > 0) | diagonal[None, :]) & inside
    limits = jnp.stack(
        [jnp.where(green_keep, partner_size, 0), jnp.broadcast_to(atom_size[:, None], (blocks, W))], axis=2
    )
    x = x_layout(three_center, offsets, keep[:rows, : blocks * W], limits.reshape(-1), packed, largest * targets)

    me = aux * n_orb + orb
    slot = jnp.arange(largest * tiles, dtype=jnp.int32) // tiles
    mine = jnp.where(slot < base, me * base + slot, targets * base + me * more + slot - base)[None, :]
    ends = jnp.pad(offsets[1:], (0, LANES - blocks * W))[:, None]
    held = (mine >= jnp.pad(offsets[:-1], (0, LANES - blocks * W))[:, None]) & (mine < ends)

    received = lax.switch(
        more,
        [functools.partial(exchange, base, most, pieces, k) for k in range(most + 1)],
        outgoing,
        x,
        kept,
    )
    held = held.astype(jnp.bfloat16)
    part = chi_part((base + more).reshape(1), left, received, held, rows, n_aux)
    whole = rows // SUB * SUB
    part = lax.all_to_all(part, "aux", split_axis=0, concat_axis=0, tiled=True)
    part = jnp.sum(part.astype(jnp.float32), axis=0).astype(jnp.bfloat16)
    part = jnp.concatenate(
        [
            part[: n_orb * whole].reshape(n_orb, whole, functions),
            part[n_orb * whole :].reshape(n_orb, rows - whole, functions),
        ],
        axis=1,
    )
    part = lax.all_to_all(part, "orb", split_axis=0, concat_axis=0, tiled=True)
    chi = jnp.sum(part.astype(jnp.float32), axis=0)
    chi = jnp.concatenate(
        [
            chi[:, : targets * whole].reshape(rows, targets, whole),
            chi[:, targets * whole :].reshape(rows, targets, rows - whole),
        ],
        axis=2,
    )
    return chi.reshape(rows, functions)


def solution(mesh):
    return jax.shard_map(
        body,
        mesh=mesh,
        in_specs=(
            P(("aux", "orb"), None, None, None),
            P(),
            P("aux", "orb", None),
            P("orb", None, None),
            P("orb", None, None),
            P("orb", None),
        ),
        out_specs=P(("aux", "orb"), None),
        check_vma=False,
    )
```

```python
import functools

import jax
import jax.numpy as jnp
import numpy as np
from jax import lax
from jax.experimental import pallas as pl
from jax.experimental.pallas import tpu as pltpu
from jax.sharding import PartitionSpec as P

BS = 64
R = 1
W = 3
ABS = 16
LANES = 128
SUB = 8
TILES = BS * BS // LANES
PER = LANES // BS
GROUP = 16


def unit_shape(rows):
    rest = rows % SUB
    tiles = SUB // rest if rest else 1
    return tiles, (rows // SUB) * tiles + (1 if rest else 0)


def gather(x, axis):
    count = 1
    for name in axis if isinstance(axis, tuple) else (axis,):
        count *= lax.axis_size(name)
    return lax.all_to_all(
        jnp.broadcast_to(x[None], (count,) + x.shape), axis, split_axis=0, concat_axis=0, tiled=True
    )


def write_unit(out_ref, unit, rows, load):
    tiles, pieces = unit_shape(rows)
    whole = rows // SUB
    rest = rows % SUB
    for j in range(tiles):
        for q in range(whole):
            out_ref[unit * pieces + j * whole + q] = load(j, q * SUB).astype(out_ref.dtype)
    if rest:
        place = lax.broadcasted_iota(jnp.int32, (SUB, LANES), 0) // rest
        last = load(0, whole * SUB)
        for j in range(1, tiles):
            last = jnp.where(place == j, load(j, whole * SUB - j * rest), last)
        out_ref[unit * pieces + tiles * whole] = last.astype(out_ref.dtype)


def selections():
    counts = range(BS // 2, BS + 1, SUB)
    chosen = np.zeros((len(counts), 2 * GROUP * BS // (4 * LANES), GROUP // 2 * BS, 2 * LANES), np.float32)
    for i, count in enumerate(counts):
        for k in range(chosen.shape[1]):
            start = min(2 * LANES * k // count // PER, GROUP // 4) * PER
            packed = 2 * LANES * k + np.arange(2 * LANES)
            row, column = packed // count, packed % count
            ok = (row < GROUP) & (row < start + GROUP // 2)
            chosen[i, k, ((row - start) * BS + column)[ok], np.arange(2 * LANES)[ok]] = 1
    return jnp.asarray(chosen, jnp.bfloat16)


def pack_block(n, count_ref, select_ref, rows, load, a_ref, c_ref):
    reach = a_ref.shape[0] // (W * BS // GROUP)
    for i in range(W * BS // GROUP):
        for j in range(GROUP // PER):
            a_ref[i * reach : (i + 1) * reach, j * LANES : (j + 1) * LANES] = load(
                i * (GROUP // PER) + j, reach
            ).astype(a_ref.dtype)
    count = count_ref[n]
    which = count // SUB - BS // 2 // SUB

    for k in range(select_ref.shape[1]):
        start = jnp.minimum(LANES * k // count, GROUP // 4)
        at = pl.multiple_of(start * LANES, LANES)
        out = jnp.dot(
            a_ref[:, pl.ds(at, GROUP // 2 * BS)],
            select_ref[which, k],
            preferred_element_type=jnp.float32,
        )
        for h in range(2):
            c_ref[2 * k + h] = out[:, h * LANES : (h + 1) * LANES]


def units_loop(begin, end, unit):
    fours = (end - begin) // 4

    def four(i, carry):
        for k in range(4):
            unit(begin + 4 * i + k)
        return carry

    def one(u, carry):
        unit(u)
        return carry

    lax.fori_loop(0, fours, four, 0)
    lax.fori_loop(begin + 4 * fours, end, one, 0)


def packed_load(n, d, u, tiles, count_ref, c_ref):
    reach = c_ref.shape[1] // (W * BS // GROUP)
    each = count_ref[n] * GROUP // LANES

    def load(j, p):
        tile = u * tiles + j
        group = sum((tile >= g * each).astype(jnp.int32) for g in range(1, BS // GROUP))
        at = (d * (BS // GROUP) + group) * reach + p
        return c_ref[tile - group * each, pl.ds(at, SUB), :]

    return load


def clear_tail(out_ref, begin, rows):
    _, pieces = unit_shape(rows)
    none = jnp.zeros((SUB, LANES), out_ref.dtype)

    def clear(i, carry):
        out_ref[i] = none
        return carry

    lax.fori_loop(begin * pieces, out_ref.shape[0], clear, 0)


def send_kernel(offset_ref, count_ref, t_ref, select_ref, base_ref, more_ref, wide_ref, a_ref, c_ref):
    rows, _, blocks, _ = t_ref.shape
    tiles, pieces = unit_shape(rows)
    step = W * TILES * blocks + SUB
    split = base_ref.shape[0] // pieces

    def widen(p, carry):
        for d in range(W):
            x = t_ref[p, d].astype(jnp.float32)
            for i in range(TILES):
                at = pl.multiple_of(p * step + (d * TILES + i) * blocks, SUB)
                wide_ref[pl.ds(at, blocks), :] = x[:, i * LANES : (i + 1) * LANES]
        return carry

    lax.fori_loop(0, rows, widen, 0)

    def block(n, carry):
        def rows_of(i, reach):
            return wide_ref[pl.ds(i * blocks + n, reach, stride=step), :]

        pack_block(n, count_ref, select_ref, rows, rows_of, a_ref, c_ref)
        for d in range(W):
            first = offset_ref[n * W + d]
            count = offset_ref[n * W + d + 1] - first
            turn = jnp.clip(split - first, 0, count)

            def unit(ref, begin, u):
                load = packed_load(n, d, u, tiles, count_ref, c_ref)
                write_unit(ref, first + u - begin, rows, load)

            units_loop(0, turn, functools.partial(unit, base_ref, 0))
            units_loop(turn, count, functools.partial(unit, more_ref, split))
        return carry

    lax.fori_loop(0, blocks, block, 0)
    total = offset_ref[blocks * W]
    clear_tail(base_ref, jnp.minimum(total, split), rows)
    clear_tail(more_ref, jnp.maximum(total - split, 0), rows)


def send_layout(three_center, offsets, counts, select, base_units, more_units):
    rows, blocks = three_center.shape[:2]
    _, pieces = unit_shape(rows)
    reach = rows // SUB * SUB + SUB
    return pl.pallas_call(
        send_kernel,
        in_specs=[pl.BlockSpec(memory_space=pltpu.SMEM)] * 2
        + [pl.BlockSpec(memory_space=pltpu.VMEM)] * 2,
        out_specs=[pl.BlockSpec(memory_space=pltpu.VMEM)] * 2,
        out_shape=[
            jax.ShapeDtypeStruct((units * pieces, SUB, LANES), jnp.bfloat16)
            for units in (base_units, more_units)
        ],
        scratch_shapes=[
            pltpu.VMEM((reach * (W * TILES * blocks + SUB), LANES), jnp.float32),
            pltpu.VMEM((W * BS // GROUP * reach, GROUP * BS), jnp.bfloat16),
            pltpu.VMEM((GROUP // PER, W * BS // GROUP * reach, LANES), jnp.float32),
        ],
        compiler_params=pltpu.CompilerParams(vmem_limit_bytes=48 << 20),
        cost_estimate=pl.CostEstimate(
            flops=0, bytes_accessed=three_center.size * 16, transcendentals=0
        ),
    )(offsets, counts, three_center.transpose(0, 2, 1, 3), select)


def green_factors(limit_ref, green_ref, blocks, gm_ref, z_ref, v_ref, o_ref):
    local = blocks // green_ref.shape[0]
    row = lax.broadcasted_iota(jnp.int32, (BS, LANES), 0)
    lane = lax.broadcasted_iota(jnp.int32, (BS, LANES), 1)
    for b in range(blocks * W):
        n, d = b // W, b % W
        at = (n % local * W + d) * BS
        g = green_ref[n // local, at : at + BS, :].astype(jnp.float32)
        g = jnp.where((row < limit_ref[2 * b]) & (lane % BS < limit_ref[2 * b + 1]), g, 0.0)
        gm_ref[b * BS : (b + 1) * BS, :] = g.astype(gm_ref.dtype)
        left = jnp.where(lane < BS, pltpu.roll(g, BS, 1), 0.0).astype(v_ref.dtype)
        right = jnp.where(lane >= BS, g, 0.0).astype(v_ref.dtype)
        v_ref[b, :BS, :LANES] = left
        v_ref[b, :BS, LANES:] = right
        v_ref[b, BS:, :LANES] = right
        v_ref[b, BS:, LANES:] = left
    pick = (lane == row % TILES * PER + row // TILES).astype(gm_ref.dtype)
    turned = lax.dot_general(
        pick, gm_ref[...], (((1,), (1,)), ((), ())), preferred_element_type=jnp.float32
    ).astype(gm_ref.dtype)
    pairs = blocks * W // PER
    stacked = jnp.concatenate([turned[:, c * LANES : (c + 1) * LANES] for c in range(pairs)], axis=0)
    into = lax.broadcasted_iota(jnp.int32, (LANES, LANES), 1)
    source = into // BS * BS + into % TILES * PER + into % BS // TILES
    perm = (lax.broadcasted_iota(jnp.int32, (LANES, LANES), 0) == source).astype(gm_ref.dtype)
    z_ref[...] = jnp.dot(stacked, perm, preferred_element_type=jnp.float32).astype(z_ref.dtype)
    o_ref[...] = jnp.zeros(o_ref.shape, o_ref.dtype)
    for n in range(blocks):
        for p in range(PER):
            for d in range(W):
                m = n + d - R
                if m < 0 or m >= blocks:
                    continue
                to = (p * W + d) * TILES
                for h in range(PER):
                    for e in range(W):
                        if abs(e - d) <= R:
                            b = m * W + e - d + R
                            line = b // PER * BS + p * TILES
                            at = b % PER * BS + (p + h) % PER * TILES
                            col = (h * W + e) * TILES
                            o_ref[n, to : to + TILES, col : col + TILES] = z_ref[
                                line : line + TILES, at : at + TILES
                            ]


def x_kernel(
    offset_ref, count_ref, keep_ref, limit_ref, t_ref, green_ref, select_ref, out_ref,
    wide_ref, t2_ref, second_ref, x_ref, gm_ref, z_ref, v_ref, o_ref, a_ref, c_ref,
):
    rows, _, blocks, _ = t_ref.shape
    tiles, _ = unit_shape(rows)
    depth = W * TILES
    green_factors(limit_ref, green_ref, blocks, gm_ref, z_ref, v_ref, o_ref)

    def turn(p, carry):
        for d in range(W):
            x = t_ref[p, d].astype(jnp.float32)
            for i in range(TILES):
                wide_ref[i * blocks : (i + 1) * blocks, :] = x[:, i * LANES : (i + 1) * LANES]
            for n in range(blocks):
                kept = wide_ref[pl.ds(n, TILES, stride=blocks), :] * keep_ref[p, n * W + d]
                at = pl.multiple_of(p * TILES, TILES)
                t2_ref[n * W + d, pl.ds(at, TILES), :] = kept.astype(t2_ref.dtype)
        return carry

    lax.fori_loop(0, rows, turn, 0)
    lane = lax.broadcasted_iota(jnp.int32, (1, LANES), 1)

    def block(n, carry):
        for e in range(W):
            total = None
            for d in range(W):
                if abs(e - d) <= R:
                    m = jnp.clip(n + d - R, 0, blocks - 1)
                    part = jnp.dot(
                        t2_ref[m * W + e - d + R], v_ref[n * W + d], preferred_element_type=jnp.float32
                    )
                    total = part if total is None else total + part
            total = total.astype(second_ref.dtype)
            for p in range(rows):
                for h in range(PER):
                    at = h * depth + e * TILES
                    second_ref[at : at + TILES, p * LANES : (p + 1) * LANES] = total[
                        p * TILES : (p + 1) * TILES, h * LANES : (h + 1) * LANES
                    ]
        chunk = 5 if rows % 5 == 0 else 1
        for c in range(rows // chunk):
            both = jnp.dot(
                o_ref[n],
                second_ref[:, c * chunk * LANES : (c + 1) * chunk * LANES],
                preferred_element_type=jnp.float32,
            )
            for i in range(chunk):
                p = c * chunk + i
                at = slice(i * LANES, (i + 1) * LANES)
                x_ref[p * (depth + 1) : p * (depth + 1) + depth, :] = jnp.where(
                    lane < BS, both[:depth, at], both[depth:, at]
                )
        def rows_of(i, reach):
            return x_ref[pl.ds(i, reach, stride=depth + 1), :]

        pack_block(n, count_ref, select_ref, rows, rows_of, a_ref, c_ref)
        for d in range(W):
            first = offset_ref[n * W + d]

            def unit(u):
                load = packed_load(n, d, u, tiles, count_ref, c_ref)
                write_unit(out_ref, first + u, rows, load)

            units_loop(0, offset_ref[n * W + d + 1] - first, unit)
        return carry

    lax.fori_loop(0, blocks, block, 0)
    clear_tail(out_ref, offset_ref[blocks * W], rows)


def x_layout(three_center, offsets, counts, keep, limits, green, select, units):
    rows, blocks = three_center.shape[:2]
    _, pieces = unit_shape(rows)
    depth = W * TILES
    reach = rows // SUB * SUB + SUB
    return pl.pallas_call(
        x_kernel,
        in_specs=[pl.BlockSpec(memory_space=pltpu.SMEM)] * 4
        + [pl.BlockSpec(memory_space=pltpu.VMEM)] * 3,
        out_specs=pl.BlockSpec(memory_space=pltpu.VMEM),
        out_shape=jax.ShapeDtypeStruct((units * pieces, SUB, LANES), jnp.bfloat16),
        scratch_shapes=[
            pltpu.VMEM((TILES * blocks, LANES), jnp.float32),
            pltpu.VMEM((blocks * W, rows * TILES, LANES), jnp.bfloat16),
            pltpu.VMEM((PER * depth, rows * LANES), jnp.bfloat16),
            pltpu.VMEM((reach * (depth + 1), LANES), jnp.float32),
            pltpu.VMEM((blocks * W * BS, LANES), jnp.bfloat16),
            pltpu.VMEM((blocks * W // PER * BS, LANES), jnp.bfloat16),
            pltpu.VMEM((blocks * W, LANES, PER * LANES), jnp.bfloat16),
            pltpu.VMEM((blocks, PER * depth, PER * depth), jnp.bfloat16),
            pltpu.VMEM((W * BS // GROUP * reach, GROUP * BS), jnp.bfloat16),
            pltpu.VMEM((GROUP // PER, W * BS // GROUP * reach, LANES), jnp.float32),
        ],
        compiler_params=pltpu.CompilerParams(vmem_limit_bytes=48 << 20),
        cost_estimate=pl.CostEstimate(
            flops=blocks * rows * (7 * TILES * LANES * LANES * 4 + 16 * TILES * TILES * 9 * LANES),
            bytes_accessed=three_center.size * 8,
            transcendentals=0,
        ),
    )(offsets, counts, keep, limits, three_center.transpose(0, 2, 1, 3), green, select)


def exchange_kernel(base, more, most, more_ref, x_ref, keep_ref, out_ref, send_sem, recv_sem, own_sem):
    n_aux, n_orb = lax.axis_size("aux"), lax.axis_size("orb")
    targets = n_aux * n_orb
    aux, orb = lax.axis_index("aux"), lax.axis_index("orb")
    me = aux * n_orb + orb

    def spans(t, source):
        yield keep_ref, out_ref.at[source, pl.ds(2 * most + base, keep_ref.shape[0])]
        yield x_ref.at[pl.ds(t * base, base)], out_ref.at[source, pl.ds(most, base)]
        if more:
            at = pl.ds(targets * base + t * more, more)
            yield x_ref.at[at], out_ref.at[source, pl.ds(most + base, more)]
            yield more_ref.at[pl.ds(t * more, more)], out_ref.at[source, pl.ds(0, more)]

    def partner(i):
        return lax.rem(aux + lax.rem(i, n_aux), n_aux), lax.rem(orb + i // n_aux + n_orb // 2, n_orb)

    def copies(t, source, to):
        return [
            pltpu.make_async_remote_copy(
                src_ref=src,
                dst_ref=dst,
                send_sem=send_sem.at[k, t],
                recv_sem=recv_sem.at[k, source],
                device_id=to,
                device_id_type=pl.DeviceIdType.MESH,
            )
            for k, (src, dst) in enumerate(spans(t, source))
        ]

    def start(i, carry):
        to = partner(i)
        t = to[0] * n_orb + to[1]

        @pl.when(t != me)
        def _():
            for copy in copies(t, me, to):
                copy.start()

        return carry

    lax.fori_loop(0, targets, start, 0)
    own = [
        pltpu.make_async_copy(src, dst, own_sem.at[k]) for k, (src, dst) in enumerate(spans(me, me))
    ]
    for copy in own:
        copy.start()

    def finish(i, carry):
        to = partner(i)
        t = to[0] * n_orb + to[1]

        @pl.when(t != me)
        def _():
            for copy in copies(t, t, to):
                copy.wait_recv()
                copy.wait_send()

        return carry

    lax.fori_loop(0, targets, finish, 0)
    for copy in own:
        copy.wait()


def exchange(base, most, pieces, more, outgoing, x, keep):
    targets = lax.axis_size("aux") * lax.axis_size("orb")
    return pl.pallas_call(
        functools.partial(exchange_kernel, base * pieces, more * pieces, most * pieces),
        in_specs=[pl.BlockSpec(memory_space=pl.ANY)] * 3,
        out_specs=pl.BlockSpec(memory_space=pl.ANY),
        out_shape=jax.ShapeDtypeStruct(
            (targets, (2 * most + base) * pieces + keep.shape[0], SUB, LANES), jnp.bfloat16
        ),
        scratch_shapes=[
            pltpu.SemaphoreType.DMA((4, targets)),
            pltpu.SemaphoreType.DMA((4, targets)),
            pltpu.SemaphoreType.DMA((4,)),
        ],
        compiler_params=pltpu.CompilerParams(has_side_effects=True),
    )(outgoing, x, keep)


def chi_kernel(rows, share_ref, left_ref, both_ref, held_ref, out_ref, l_ref, r_ref, k_ref):
    sources = left_ref.shape[0]
    tiles, pieces = unit_shape(rows)
    base = left_ref.shape[1] // pieces
    most = (both_ref.shape[1] // pieces - base) // 2
    whole, rest = rows // SUB, rows % SUB
    main = sources * whole * SUB

    def assemble(from_ref, first, to_ref, u, tiles=tiles):
        for j in range(tiles):
            at = slice((u * tiles + j) * LANES, (u * tiles + j + 1) * LANES)
            for s in range(sources):
                if whole:
                    i = first + j * whole
                    to_ref[s * whole * SUB : (s + 1) * whole * SUB, at] = jnp.concatenate(
                        [from_ref[s, i + q] for q in range(whole)], axis=0
                    )
            if rest:
                i = first + tiles * whole
                step = SUB // rest
                for s in range(0, sources, step):
                    to_ref[main + s * rest : main + (s + step) * rest, at] = jnp.concatenate(
                        [from_ref[s + t, i, j * rest : (j + 1) * rest, :] for t in range(step)],
                        axis=0,
                    )

    assemble(both_ref, (2 * most + base) * pieces, k_ref, 0, 1)
    keep = jnp.dot(k_ref[...], held_ref[...], preferred_element_type=jnp.float32)
    keep = keep.astype(l_ref.dtype)

    def fill(u):
        if u < base:
            assemble(left_ref, u * pieces, l_ref, u)
        else:
            assemble(both_ref, (u - base) * pieces, l_ref, u)
        assemble(both_ref, (most + u) * pieces, r_ref, u)
        for i in range(u * tiles, (u + 1) * tiles):
            at = slice(i * LANES, (i + 1) * LANES)
            l_ref[:, at] = l_ref[:, at] * keep[:, i : i + 1]

    def clear(u):
        at = slice(u * tiles * LANES, (u + 1) * tiles * LANES)
        l_ref[:, at] = jnp.zeros((l_ref.shape[0], tiles * LANES), l_ref.dtype)
        r_ref[:, at] = jnp.zeros((r_ref.shape[0], tiles * LANES), r_ref.dtype)

    for u in range(base + most):
        if u < base:
            fill(u)
        else:
            pl.when(u < share_ref[0])(functools.partial(fill, u))
            pl.when(u >= share_ref[0])(functools.partial(clear, u))
    chi = lax.dot_general(
        l_ref[...], r_ref[...], (((1,), (1,)), ((), ())), preferred_element_type=jnp.float32
    ).astype(out_ref.dtype)
    groups, height = out_ref.shape[:2]
    top = main // groups
    for a in range(groups):
        out_ref[a, :top, :] = chi[a * top : (a + 1) * top]
        if rest:
            low = height - top
            out_ref[a, top:, :] = chi[main + a * low : main + (a + 1) * low]


def chi_part(share, left, both, held, rows, groups):
    sources = left.shape[0]
    tiles, pieces = unit_shape(rows)
    functions = sources * rows
    units = (left.shape[1] // pieces + both.shape[1] // pieces) // 2
    depth = units * tiles * LANES
    return pl.pallas_call(
        functools.partial(chi_kernel, rows),
        in_specs=[pl.BlockSpec(memory_space=pltpu.SMEM)]
        + [pl.BlockSpec(memory_space=pltpu.VMEM)] * 3,
        out_specs=pl.BlockSpec(memory_space=pltpu.VMEM),
        out_shape=jax.ShapeDtypeStruct((groups, functions // groups, functions), jnp.bfloat16),
        scratch_shapes=[pltpu.VMEM((functions, k), jnp.bfloat16) for k in (depth, depth, LANES)],
        compiler_params=pltpu.CompilerParams(vmem_limit_bytes=56 << 20),
    )(share, left, both, held)


def body(three_center, atom_size, tensor_pattern, green_occ, green_virt, green_pattern):
    both = ("aux", "orb")
    n_aux, n_orb = lax.axis_size("aux"), lax.axis_size("orb")
    aux, orb = lax.axis_index("aux"), lax.axis_index("orb")
    rows, blocks = three_center.shape[0], three_center.shape[1]
    local_blocks = green_occ.shape[0]
    area = BS * BS
    targets = n_aux * n_orb
    functions = targets * rows
    tiles, pieces = unit_shape(rows)

    owned = jnp.arange(blocks, dtype=jnp.int32)[:, None]
    partner = owned + jnp.arange(W, dtype=jnp.int32)[None, :] - R
    inside = (partner >= 0) & (partner < blocks)
    catalog = jnp.arange(blocks, dtype=jnp.int32)
    partner_size = jnp.sum(jnp.where(partner[:, :, None] == catalog, atom_size, 0), axis=2)
    counts = jnp.clip(-(-atom_size // SUB) * SUB, BS // 2, BS)
    taken = -(-partner_size * counts[:, None] // (tiles * LANES)) * inside
    select = selections()
    before = jnp.arange(blocks * W + 1, dtype=jnp.int32)[:, None]
    before = before > jnp.arange(blocks * W, dtype=jnp.int32)[None, :]
    offsets = jnp.sum(jnp.where(before, taken.reshape(1, -1), 0), axis=1).astype(jnp.int32)
    largest = -(-(blocks * W - 2 * R) * TILES // (tiles * targets))
    base = -(-largest // 2)
    most = largest - base
    more = jnp.clip(-(-offsets[-1] // targets) - base, 0, most)

    groups = tensor_pattern.shape[0]
    flags = [tensor_pattern.transpose(1, 2, 0).reshape(local_blocks * W, groups)]
    flags.append(green_pattern.reshape(local_blocks * W, 1))
    flags = (jnp.concatenate(flags, axis=1) > 0).astype(jnp.bfloat16)
    lines = -(-local_blocks * W // SUB) * SUB
    flags = jnp.pad(flags, ((0, lines - local_blocks * W), (0, LANES - groups - 1)))
    square = (local_blocks * W * BS, BS)
    packed = jnp.concatenate([green_occ.reshape(square), green_virt.reshape(square)], axis=1)
    packed = gather(jnp.concatenate([packed, flags], axis=0), "orb")

    first, outgoing = send_layout(three_center, offsets, counts, select, base * targets, most * targets)
    packed, first = lax.optimization_barrier((packed, first))
    left = lax.all_to_all(
        first.reshape(targets, base * pieces, SUB, LANES), both, split_axis=0, concat_axis=0, tiled=True
    )

    flags = packed[:, square[0] : square[0] + local_blocks * W, :].reshape(blocks * W, LANES)
    mine = (orb * rows + jnp.arange(pieces * SUB, dtype=jnp.int32)) // ABS
    wanted = mine[:, None] == jnp.arange(LANES, dtype=jnp.int32)[None, :]
    keep = lax.dot_general(
        wanted.astype(flags.dtype),
        jnp.pad(flags, ((0, LANES - blocks * W), (0, 0))),
        (((1,), (1,)), ((), ())),
        preferred_element_type=jnp.float32,
    )
    held_pieces = rows // SUB + (1 if rows % SUB else 0)
    kept = keep[: held_pieces * SUB].astype(jnp.bfloat16).reshape(held_pieces, SUB, LANES)

    diagonal = jnp.arange(W, dtype=jnp.int32) == R
    green_all = flags[:, groups].reshape(blocks, W)
    green_keep = ((green_all > 0) | diagonal[None, :]) & inside
    limits = jnp.stack(
        [jnp.where(green_keep, partner_size, 0), jnp.broadcast_to(atom_size[:, None], (blocks, W))], axis=2
    )
    x = x_layout(
        three_center, offsets, counts, keep[:rows, : blocks * W], limits.reshape(-1), packed, select, largest * targets
    )

    me = aux * n_orb + orb
    slot = jnp.arange(largest * tiles, dtype=jnp.int32) // tiles
    mine = jnp.where(slot < base, me * base + slot, targets * base + me * more + slot - base)[None, :]
    ends = jnp.pad(offsets[1:], (0, LANES - blocks * W))[:, None]
    held = (mine >= jnp.pad(offsets[:-1], (0, LANES - blocks * W))[:, None]) & (mine < ends)

    received = lax.switch(
        more,
        [functools.partial(exchange, base, most, pieces, k) for k in range(most + 1)],
        outgoing,
        x,
        kept,
    )
    held = held.astype(jnp.bfloat16)
    part = chi_part((base + more).reshape(1), left, received, held, rows, n_aux)
    whole = rows // SUB * SUB
    part = lax.all_to_all(part, "aux", split_axis=0, concat_axis=0, tiled=True)
    part = jnp.sum(part.astype(jnp.float32), axis=0).astype(jnp.bfloat16)
    part = jnp.concatenate(
        [
            part[: n_orb * whole].reshape(n_orb, whole, functions),
            part[n_orb * whole :].reshape(n_orb, rows - whole, functions),
        ],
        axis=1,
    )
    part = lax.all_to_all(part, "orb", split_axis=0, concat_axis=0, tiled=True)
    chi = jnp.sum(part.astype(jnp.float32), axis=0)
    chi = jnp.concatenate(
        [
            chi[:, : targets * whole].reshape(rows, targets, whole),
            chi[:, targets * whole :].reshape(rows, targets, rows - whole),
        ],
        axis=2,
    )
    return chi.reshape(rows, functions)


def solution(mesh):
    return jax.shard_map(
        body,
        mesh=mesh,
        in_specs=(
            P(("aux", "orb"), None, None, None),
            P(),
            P("aux", "orb", None),
            P("orb", None, None),
            P("orb", None, None),
            P("orb", None),
        ),
        out_specs=P(("aux", "orb"), None),
        check_vma=False,
    )
```

```python
import functools

import jax
import jax.numpy as jnp
import numpy as np
from jax import lax
from jax.experimental import pallas as pl
from jax.experimental.pallas import tpu as pltpu
from jax.sharding import PartitionSpec as P

BS = 64
R = 1
W = 3
ABS = 16
LANES = 128
SUB = 8
TILES = BS * BS // LANES
PER = LANES // BS
GROUP = 16


def unit_shape(rows):
    rest = rows % SUB
    tiles = SUB // rest if rest else 1
    return tiles, (rows // SUB) * tiles + (1 if rest else 0)


def gather(x, axis):
    count = 1
    for name in axis if isinstance(axis, tuple) else (axis,):
        count *= lax.axis_size(name)
    return lax.all_to_all(
        jnp.broadcast_to(x[None], (count,) + x.shape), axis, split_axis=0, concat_axis=0, tiled=True
    )


def write_unit(out_ref, unit, rows, load):
    tiles, pieces = unit_shape(rows)
    whole = rows // SUB
    rest = rows % SUB
    for j in range(tiles):
        for q in range(whole):
            out_ref[unit * pieces + j * whole + q] = load(j, q * SUB).astype(out_ref.dtype)
    if rest:
        place = lax.broadcasted_iota(jnp.int32, (SUB, LANES), 0) // rest
        last = load(0, whole * SUB)
        for j in range(1, tiles):
            last = jnp.where(place == j, load(j, whole * SUB - j * rest), last)
        out_ref[unit * pieces + tiles * whole] = last.astype(out_ref.dtype)


def selections():
    counts = range(BS // 2, BS + 1, SUB)
    chosen = np.zeros((len(counts), 2 * GROUP * BS // (4 * LANES), GROUP // 2 * BS, 2 * LANES), np.float32)
    for i, count in enumerate(counts):
        for k in range(chosen.shape[1]):
            start = min(2 * LANES * k // count // PER, GROUP // 4) * PER
            packed = 2 * LANES * k + np.arange(2 * LANES)
            row, column = packed // count, packed % count
            ok = (row < GROUP) & (row < start + GROUP // 2)
            chosen[i, k, ((row - start) * BS + column)[ok], np.arange(2 * LANES)[ok]] = 1
    return jnp.asarray(chosen, jnp.bfloat16)


def pack_block(n, count_ref, select_ref, rows, load, a_ref, c_ref):
    reach = a_ref.shape[0] // (W * BS // GROUP)
    for i in range(W * BS // GROUP):
        for j in range(GROUP // PER):
            a_ref[i * reach : (i + 1) * reach, j * LANES : (j + 1) * LANES] = load(
                i * (GROUP // PER) + j, reach
            ).astype(a_ref.dtype)
    count = count_ref[n]
    which = count // SUB - BS // 2 // SUB

    for k in range(select_ref.shape[1]):
        start = jnp.minimum(LANES * k // count, GROUP // 4)
        at = pl.multiple_of(start * LANES, LANES)
        out = jnp.dot(
            a_ref[:, pl.ds(at, GROUP // 2 * BS)],
            select_ref[which, k],
            preferred_element_type=jnp.float32,
        )
        for h in range(2):
            c_ref[2 * k + h] = out[:, h * LANES : (h + 1) * LANES]


def units_loop(begin, end, unit):
    fours = (end - begin) // 4

    def four(i, carry):
        for k in range(4):
            unit(begin + 4 * i + k)
        return carry

    def one(u, carry):
        unit(u)
        return carry

    lax.fori_loop(0, fours, four, 0)
    lax.fori_loop(begin + 4 * fours, end, one, 0)


def packed_load(n, d, u, tiles, count_ref, c_ref):
    reach = c_ref.shape[1] // (W * BS // GROUP)
    each = count_ref[n] * GROUP // LANES

    def load(j, p):
        tile = u * tiles + j
        group = sum((tile >= g * each).astype(jnp.int32) for g in range(1, BS // GROUP))
        at = (d * (BS // GROUP) + group) * reach + p
        return c_ref[tile - group * each, pl.ds(at, SUB), :]

    return load


def clear_tail(out_ref, begin, rows):
    _, pieces = unit_shape(rows)
    none = jnp.zeros((SUB, LANES), out_ref.dtype)

    def clear(i, carry):
        out_ref[i] = none
        return carry

    lax.fori_loop(begin * pieces, out_ref.shape[0], clear, 0)


def send_kernel(offset_ref, count_ref, t_ref, select_ref, base_ref, more_ref, wide_ref, a_ref, c_ref):
    rows, _, blocks, _ = t_ref.shape
    tiles, pieces = unit_shape(rows)
    step = W * TILES * blocks + SUB
    split = base_ref.shape[0] // pieces

    def widen(p, carry):
        for d in range(W):
            x = t_ref[p, d].astype(jnp.float32)
            for i in range(TILES):
                at = pl.multiple_of(p * step + (d * TILES + i) * blocks, SUB)
                wide_ref[pl.ds(at, blocks), :] = x[:, i * LANES : (i + 1) * LANES]
        return carry

    lax.fori_loop(0, rows, widen, 0)

    def block(n, carry):
        def rows_of(i, reach):
            return wide_ref[pl.ds(i * blocks + n, reach, stride=step), :]

        pack_block(n, count_ref, select_ref, rows, rows_of, a_ref, c_ref)
        for d in range(W):
            first = offset_ref[n * W + d]
            count = offset_ref[n * W + d + 1] - first
            turn = jnp.clip(split - first, 0, count)

            def unit(ref, begin, u):
                load = packed_load(n, d, u, tiles, count_ref, c_ref)
                write_unit(ref, first + u - begin, rows, load)

            units_loop(0, turn, functools.partial(unit, base_ref, 0))
            units_loop(turn, count, functools.partial(unit, more_ref, split))
        return carry

    lax.fori_loop(0, blocks, block, 0)
    total = offset_ref[blocks * W]
    clear_tail(base_ref, jnp.minimum(total, split), rows)
    clear_tail(more_ref, jnp.maximum(total - split, 0), rows)


def send_layout(three_center, offsets, counts, select, base_units, more_units):
    rows, blocks = three_center.shape[:2]
    _, pieces = unit_shape(rows)
    reach = rows // SUB * SUB + SUB
    return pl.pallas_call(
        send_kernel,
        in_specs=[pl.BlockSpec(memory_space=pltpu.SMEM)] * 2
        + [pl.BlockSpec(memory_space=pltpu.VMEM)] * 2,
        out_specs=[pl.BlockSpec(memory_space=pltpu.VMEM)] * 2,
        out_shape=[
            jax.ShapeDtypeStruct((units * pieces, SUB, LANES), jnp.bfloat16)
            for units in (base_units, more_units)
        ],
        scratch_shapes=[
            pltpu.VMEM((reach * (W * TILES * blocks + SUB), LANES), jnp.float32),
            pltpu.VMEM((W * BS // GROUP * reach, GROUP * BS), jnp.bfloat16),
            pltpu.VMEM((GROUP // PER, W * BS // GROUP * reach, LANES), jnp.float32),
        ],
        compiler_params=pltpu.CompilerParams(vmem_limit_bytes=48 << 20),
        cost_estimate=pl.CostEstimate(
            flops=0, bytes_accessed=three_center.size * 16, transcendentals=0
        ),
    )(offsets, counts, three_center.transpose(0, 2, 1, 3), select)


def green_factors(limit_ref, green_ref, blocks, gm_ref, z_ref, v_ref, o_ref):
    local = blocks // green_ref.shape[0]
    row = lax.broadcasted_iota(jnp.int32, (BS, LANES), 0)
    lane = lax.broadcasted_iota(jnp.int32, (BS, LANES), 1)
    for b in range(blocks * W):
        n, d = b // W, b % W
        at = (n % local * W + d) * BS
        g = green_ref[n // local, at : at + BS, :].astype(jnp.float32)
        g = jnp.where((row < limit_ref[2 * b]) & (lane % BS < limit_ref[2 * b + 1]), g, 0.0)
        gm_ref[b * BS : (b + 1) * BS, :] = g.astype(gm_ref.dtype)
        left = jnp.where(lane < BS, pltpu.roll(g, BS, 1), 0.0).astype(v_ref.dtype)
        right = jnp.where(lane >= BS, g, 0.0).astype(v_ref.dtype)
        v_ref[b, :BS, :LANES] = left
        v_ref[b, :BS, LANES:] = right
        v_ref[b, BS:, :LANES] = right
        v_ref[b, BS:, LANES:] = left
    pick = (lane == row % TILES * PER + row // TILES).astype(gm_ref.dtype)
    turned = lax.dot_general(
        pick, gm_ref[...], (((1,), (1,)), ((), ())), preferred_element_type=jnp.float32
    ).astype(gm_ref.dtype)
    pairs = blocks * W // PER
    stacked = jnp.concatenate([turned[:, c * LANES : (c + 1) * LANES] for c in range(pairs)], axis=0)
    into = lax.broadcasted_iota(jnp.int32, (LANES, LANES), 1)
    source = into // BS * BS + into % TILES * PER + into % BS // TILES
    perm = (lax.broadcasted_iota(jnp.int32, (LANES, LANES), 0) == source).astype(gm_ref.dtype)
    z_ref[...] = jnp.dot(stacked, perm, preferred_element_type=jnp.float32).astype(z_ref.dtype)
    o_ref[...] = jnp.zeros(o_ref.shape, o_ref.dtype)
    for n in range(blocks):
        for p in range(PER):
            for d in range(W):
                m = n + d - R
                if m < 0 or m >= blocks:
                    continue
                to = (p * W + d) * TILES
                for h in range(PER):
                    for e in range(W):
                        if abs(e - d) <= R:
                            b = m * W + e - d + R
                            line = b // PER * BS + p * TILES
                            at = b % PER * BS + (p + h) % PER * TILES
                            col = (h * W + e) * TILES
                            o_ref[n, to : to + TILES, col : col + TILES] = z_ref[
                                line : line + TILES, at : at + TILES
                            ]


def x_kernel(
    offset_ref, count_ref, keep_ref, limit_ref, t_ref, green_ref, select_ref, out_ref,
    wide_ref, t2_ref, second_ref, x_ref, gm_ref, z_ref, v_ref, o_ref, a_ref, c_ref,
):
    rows, _, blocks, _ = t_ref.shape
    tiles, _ = unit_shape(rows)
    depth = W * TILES
    green_factors(limit_ref, green_ref, blocks, gm_ref, z_ref, v_ref, o_ref)

    def turn(p, carry):
        for d in range(W):
            x = t_ref[p, d].astype(jnp.float32)
            for i in range(TILES):
                wide_ref[i * blocks : (i + 1) * blocks, :] = x[:, i * LANES : (i + 1) * LANES]
            for n in range(blocks):
                kept = wide_ref[pl.ds(n, TILES, stride=blocks), :] * keep_ref[p, n * W + d]
                at = pl.multiple_of(p * TILES, TILES)
                t2_ref[n * W + d, pl.ds(at, TILES), :] = kept.astype(t2_ref.dtype)
        return carry

    lax.fori_loop(0, rows, turn, 0)
    lane = lax.broadcasted_iota(jnp.int32, (1, LANES), 1)

    def block(n, carry):
        for e in range(W):
            total = None
            for d in range(W):
                if abs(e - d) <= R:
                    m = jnp.clip(n + d - R, 0, blocks - 1)
                    part = jnp.dot(
                        t2_ref[m * W + e - d + R], v_ref[n * W + d], preferred_element_type=jnp.float32
                    )
                    total = part if total is None else total + part
            total = total.astype(second_ref.dtype)
            for p in range(rows):
                for h in range(PER):
                    at = h * depth + e * TILES
                    second_ref[at : at + TILES, p * LANES : (p + 1) * LANES] = total[
                        p * TILES : (p + 1) * TILES, h * LANES : (h + 1) * LANES
                    ]
        chunk = 5 if rows % 5 == 0 else 1
        for c in range(rows // chunk):
            both = jnp.dot(
                o_ref[n],
                second_ref[:, c * chunk * LANES : (c + 1) * chunk * LANES],
                preferred_element_type=jnp.float32,
            )
            for i in range(chunk):
                p = c * chunk + i
                at = slice(i * LANES, (i + 1) * LANES)
                x_ref[p * (depth + 1) : p * (depth + 1) + depth, :] = jnp.where(
                    lane < BS, both[:depth, at], both[depth:, at]
                )
        def rows_of(i, reach):
            return x_ref[pl.ds(i, reach, stride=depth + 1), :]

        pack_block(n, count_ref, select_ref, rows, rows_of, a_ref, c_ref)
        for d in range(W):
            first = offset_ref[n * W + d]

            def unit(u):
                load = packed_load(n, d, u, tiles, count_ref, c_ref)
                write_unit(out_ref, first + u, rows, load)

            units_loop(0, offset_ref[n * W + d + 1] - first, unit)
        return carry

    lax.fori_loop(0, blocks, block, 0)
    clear_tail(out_ref, offset_ref[blocks * W], rows)


def x_layout(three_center, offsets, counts, keep, limits, green, select, units):
    rows, blocks = three_center.shape[:2]
    _, pieces = unit_shape(rows)
    depth = W * TILES
    reach = rows // SUB * SUB + SUB
    return pl.pallas_call(
        x_kernel,
        in_specs=[pl.BlockSpec(memory_space=pltpu.SMEM)] * 4
        + [pl.BlockSpec(memory_space=pltpu.VMEM)] * 3,
        out_specs=pl.BlockSpec(memory_space=pltpu.VMEM),
        out_shape=jax.ShapeDtypeStruct((units * pieces, SUB, LANES), jnp.bfloat16),
        scratch_shapes=[
            pltpu.VMEM((TILES * blocks, LANES), jnp.float32),
            pltpu.VMEM((blocks * W, rows * TILES, LANES), jnp.bfloat16),
            pltpu.VMEM((PER * depth, rows * LANES), jnp.bfloat16),
            pltpu.VMEM((reach * (depth + 1), LANES), jnp.float32),
            pltpu.VMEM((blocks * W * BS, LANES), jnp.bfloat16),
            pltpu.VMEM((blocks * W // PER * BS, LANES), jnp.bfloat16),
            pltpu.VMEM((blocks * W, LANES, PER * LANES), jnp.bfloat16),
            pltpu.VMEM((blocks, PER * depth, PER * depth), jnp.bfloat16),
            pltpu.VMEM((W * BS // GROUP * reach, GROUP * BS), jnp.bfloat16),
            pltpu.VMEM((GROUP // PER, W * BS // GROUP * reach, LANES), jnp.float32),
        ],
        compiler_params=pltpu.CompilerParams(vmem_limit_bytes=48 << 20),
        cost_estimate=pl.CostEstimate(
            flops=blocks * rows * (7 * TILES * LANES * LANES * 4 + 16 * TILES * TILES * 9 * LANES),
            bytes_accessed=three_center.size * 8,
            transcendentals=0,
        ),
    )(offsets, counts, keep, limits, three_center.transpose(0, 2, 1, 3), green, select)


def exchange_kernel(base, more, most, more_ref, x_ref, keep_ref, out_ref, send_sem, recv_sem, own_sem):
    n_aux, n_orb = lax.axis_size("aux"), lax.axis_size("orb")
    targets = n_aux * n_orb
    aux, orb = lax.axis_index("aux"), lax.axis_index("orb")
    me = aux * n_orb + orb

    def spans(t, source):
        yield keep_ref, out_ref.at[source, pl.ds(2 * most + base, keep_ref.shape[0])]
        yield x_ref.at[pl.ds(t * base, base)], out_ref.at[source, pl.ds(most, base)]
        if more:
            at = pl.ds(targets * base + t * more, more)
            yield x_ref.at[at], out_ref.at[source, pl.ds(most + base, more)]
            yield more_ref.at[pl.ds(t * more, more)], out_ref.at[source, pl.ds(0, more)]

    def partner(i):
        return lax.rem(aux + lax.rem(i, n_aux), n_aux), lax.rem(orb + i // n_aux + n_orb // 2, n_orb)

    def copies(t, source, to):
        return [
            pltpu.make_async_remote_copy(
                src_ref=src,
                dst_ref=dst,
                send_sem=send_sem.at[k, t],
                recv_sem=recv_sem.at[k, source],
                device_id=to,
                device_id_type=pl.DeviceIdType.MESH,
            )
            for k, (src, dst) in enumerate(spans(t, source))
        ]

    def start(i, carry):
        to = partner(i)
        t = to[0] * n_orb + to[1]

        @pl.when(t != me)
        def _():
            for copy in copies(t, me, to):
                copy.start()

        return carry

    lax.fori_loop(0, targets, start, 0)
    own = [
        pltpu.make_async_copy(src, dst, own_sem.at[k]) for k, (src, dst) in enumerate(spans(me, me))
    ]
    for copy in own:
        copy.start()

    def finish(i, carry):
        to = partner(i)
        t = to[0] * n_orb + to[1]

        @pl.when(t != me)
        def _():
            for copy in copies(t, t, to):
                copy.wait_recv()
                copy.wait_send()

        return carry

    lax.fori_loop(0, targets, finish, 0)
    for copy in own:
        copy.wait()


def exchange(base, most, pieces, more, outgoing, x, keep):
    targets = lax.axis_size("aux") * lax.axis_size("orb")
    return pl.pallas_call(
        functools.partial(exchange_kernel, base * pieces, more * pieces, most * pieces),
        in_specs=[pl.BlockSpec(memory_space=pl.ANY)] * 3,
        out_specs=pl.BlockSpec(memory_space=pl.ANY),
        out_shape=jax.ShapeDtypeStruct(
            (targets, (2 * most + base) * pieces + keep.shape[0], SUB, LANES), jnp.bfloat16
        ),
        scratch_shapes=[
            pltpu.SemaphoreType.DMA((4, targets)),
            pltpu.SemaphoreType.DMA((4, targets)),
            pltpu.SemaphoreType.DMA((4,)),
        ],
        compiler_params=pltpu.CompilerParams(has_side_effects=True),
    )(outgoing, x, keep)


def chi_kernel(rows, share_ref, left_ref, both_ref, held_ref, out_ref, l_ref, r_ref, k_ref):
    sources = left_ref.shape[0]
    tiles, pieces = unit_shape(rows)
    base = left_ref.shape[1] // pieces
    most = (both_ref.shape[1] // pieces - base) // 2
    whole, rest = rows // SUB, rows % SUB
    main = sources * whole * SUB

    def assemble(from_ref, first, to_ref, u, tiles=tiles):
        for j in range(tiles):
            at = slice((u * tiles + j) * LANES, (u * tiles + j + 1) * LANES)
            for s in range(sources):
                if whole:
                    i = first + j * whole
                    to_ref[s * whole * SUB : (s + 1) * whole * SUB, at] = jnp.concatenate(
                        [from_ref[s, i + q] for q in range(whole)], axis=0
                    )
            if rest:
                i = first + tiles * whole
                step = SUB // rest
                for s in range(0, sources, step):
                    to_ref[main + s * rest : main + (s + step) * rest, at] = jnp.concatenate(
                        [from_ref[s + t, i, j * rest : (j + 1) * rest, :] for t in range(step)],
                        axis=0,
                    )

    assemble(both_ref, (2 * most + base) * pieces, k_ref, 0, 1)
    keep = jnp.dot(k_ref[...], held_ref[...], preferred_element_type=jnp.float32)
    keep = keep.astype(l_ref.dtype)

    def fill(u):
        if u < base:
            assemble(left_ref, u * pieces, l_ref, u)
        else:
            assemble(both_ref, (u - base) * pieces, l_ref, u)
        assemble(both_ref, (most + u) * pieces, r_ref, u)
        for i in range(u * tiles, (u + 1) * tiles):
            at = slice(i * LANES, (i + 1) * LANES)
            l_ref[:, at] = l_ref[:, at] * keep[:, i : i + 1]

    def clear(u):
        at = slice(u * tiles * LANES, (u + 1) * tiles * LANES)
        l_ref[:, at] = jnp.zeros((l_ref.shape[0], tiles * LANES), l_ref.dtype)
        r_ref[:, at] = jnp.zeros((r_ref.shape[0], tiles * LANES), r_ref.dtype)

    for u in range(base + most):
        if u < base:
            fill(u)
        else:
            pl.when(u < share_ref[0])(functools.partial(fill, u))
            pl.when(u >= share_ref[0])(functools.partial(clear, u))
    chi = lax.dot_general(
        l_ref[...], r_ref[...], (((1,), (1,)), ((), ())), preferred_element_type=jnp.float32
    ).astype(out_ref.dtype)
    groups, height = out_ref.shape[:2]
    top = main // groups
    for a in range(groups):
        out_ref[a, :top, :] = chi[a * top : (a + 1) * top]
        if rest:
            low = height - top
            out_ref[a, top:, :] = chi[main + a * low : main + (a + 1) * low]


def chi_part(share, left, both, held, rows, groups):
    sources = left.shape[0]
    tiles, pieces = unit_shape(rows)
    functions = sources * rows
    units = (left.shape[1] // pieces + both.shape[1] // pieces) // 2
    depth = units * tiles * LANES
    return pl.pallas_call(
        functools.partial(chi_kernel, rows),
        in_specs=[pl.BlockSpec(memory_space=pltpu.SMEM)]
        + [pl.BlockSpec(memory_space=pltpu.VMEM)] * 3,
        out_specs=pl.BlockSpec(memory_space=pltpu.VMEM),
        out_shape=jax.ShapeDtypeStruct((groups, functions // groups, functions), jnp.float32),
        scratch_shapes=[pltpu.VMEM((functions, k), jnp.bfloat16) for k in (depth, depth, LANES)],
        compiler_params=pltpu.CompilerParams(vmem_limit_bytes=56 << 20),
    )(share, left, both, held)


def total_kernel(rows, cores, chunks, part_ref, out_ref, pair_ref, left_ref, near_ref, held_ref, right_ref, far_ref, *sems):
    n_aux, n_orb = lax.axis_size("aux"), lax.axis_size("orb")
    aux, orb = lax.axis_index("aux"), lax.axis_index("orb")
    chips = n_aux // cores
    chip, core = aux // cores, lax.rem(aux, cores)
    other = cores - 1 - core
    whole, rest = rows // SUB * SUB, rows % SUB
    pair_send, pair_recv, near_send, near_recv, far_send, far_recv = sems

    def remote(src, dst, send, recv, to):
        return pltpu.make_async_remote_copy(
            src_ref=src, dst_ref=dst, send_sem=send, recv_sem=recv,
            device_id=to, device_id_type=pl.DeviceIdType.MESH,
        )

    def pair(c, i):
        to = lax.rem(chip + i, chips)
        at = chunks[c]
        return remote(
            part_ref.at[to * cores + other, :, at], pair_ref.at[to, :, at],
            pair_send.at[c, i], pair_recv.at[c, i], (chip * cores + other, orb),
        )

    def near(c, i):
        at = chunks[c]
        return remote(
            left_ref.at[i, :, at], near_ref.at[i, :, at],
            near_send.at[c, i], near_recv.at[c, i], (lax.rem(chip + i, chips) * cores + core, orb),
        )

    def far(c, i):
        to = lax.rem(orb + i, n_orb)
        at = chunks[c]
        return remote(
            right_ref.at[to, :, at], far_ref.at[i, :, at], far_send.at[c, i], far_recv.at[c, i], (aux, to)
        )

    order = list(range(1, chips)) + [0]
    for c in range(len(chunks)):
        for i in order:
            pair(c, i).start()
    for c, at in enumerate(chunks):
        for i in order:
            to = lax.rem(chip + i, chips)
            pair(c, i).wait_recv()
            both = part_ref[to * cores + core, :, at] + pair_ref[to, :, at]
            if i:
                left_ref[i, :, at] = both.astype(left_ref.dtype)
                near(c, i).start()
            else:
                held_ref[:, at] = both
    for c, at in enumerate(chunks):
        total = held_ref[:, at]
        for i in range(1, chips):
            near(c, i).wait_recv()
            total = total + near_ref[i, :, at].astype(jnp.float32)
        held_ref[:, at] = total
        for o in range(n_orb):
            right_ref[o, :whole, at] = total[o * whole : (o + 1) * whole].astype(right_ref.dtype)
            if rest:
                low = n_orb * whole + o * rest
                tail = total[low // SUB * SUB : low // SUB * SUB + SUB]
                if low % SUB:
                    tail = pltpu.roll(tail, SUB - low % SUB, 0)
                right_ref[o, whole:, at] = tail.astype(right_ref.dtype)
        for i in range(1, n_orb):
            far(c, i).start()
    for c, at in enumerate(chunks):
        total = right_ref[orb, :, at].astype(jnp.float32)
        for i in range(1, n_orb):
            far(c, i).wait_recv()
            total = total + far_ref[i, :, at].astype(jnp.float32)
        out_ref[:, at] = total
    for c in range(len(chunks)):
        for i in range(chips):
            pair(c, i).wait_send()
        for i in range(1, chips):
            near(c, i).wait_send()
        for i in range(1, n_orb):
            far(c, i).wait_send()


def total_part(part, rows):
    n_aux, height, functions = part.shape
    n_orb = lax.axis_size("orb")
    cores = 2
    chips = n_aux // cores
    tall = -(-rows // SUB) * SUB
    cut = functions // LANES // 2 * LANES
    chunks = (slice(0, cut), slice(cut, functions))
    wide = jnp.float32
    return pl.pallas_call(
        functools.partial(total_kernel, rows, cores, chunks),
        in_specs=[pl.BlockSpec(memory_space=pltpu.VMEM)],
        out_specs=pl.BlockSpec(memory_space=pltpu.VMEM),
        out_shape=jax.ShapeDtypeStruct((tall, functions), wide),
        scratch_shapes=[
            pltpu.VMEM((chips, height, functions), wide),
            pltpu.VMEM((chips, height, functions), jnp.bfloat16),
            pltpu.VMEM((chips, height, functions), jnp.bfloat16),
            pltpu.VMEM((height, functions), wide),
            pltpu.VMEM((n_orb, tall, functions), jnp.bfloat16),
            pltpu.VMEM((n_orb, tall, functions), jnp.bfloat16),
        ]
        + [pltpu.SemaphoreType.DMA((2, k)) for k in (chips, chips, chips, chips, n_orb, n_orb)],
        compiler_params=pltpu.CompilerParams(has_side_effects=True, vmem_limit_bytes=48 << 20),
    )(part)


def body(three_center, atom_size, tensor_pattern, green_occ, green_virt, green_pattern):
    both = ("aux", "orb")
    n_aux, n_orb = lax.axis_size("aux"), lax.axis_size("orb")
    aux, orb = lax.axis_index("aux"), lax.axis_index("orb")
    rows, blocks = three_center.shape[0], three_center.shape[1]
    local_blocks = green_occ.shape[0]
    area = BS * BS
    targets = n_aux * n_orb
    functions = targets * rows
    tiles, pieces = unit_shape(rows)

    owned = jnp.arange(blocks, dtype=jnp.int32)[:, None]
    partner = owned + jnp.arange(W, dtype=jnp.int32)[None, :] - R
    inside = (partner >= 0) & (partner < blocks)
    catalog = jnp.arange(blocks, dtype=jnp.int32)
    partner_size = jnp.sum(jnp.where(partner[:, :, None] == catalog, atom_size, 0), axis=2)
    counts = jnp.clip(-(-atom_size // SUB) * SUB, BS // 2, BS)
    taken = -(-partner_size * counts[:, None] // (tiles * LANES)) * inside
    select = selections()
    before = jnp.arange(blocks * W + 1, dtype=jnp.int32)[:, None]
    before = before > jnp.arange(blocks * W, dtype=jnp.int32)[None, :]
    offsets = jnp.sum(jnp.where(before, taken.reshape(1, -1), 0), axis=1).astype(jnp.int32)
    largest = -(-(blocks * W - 2 * R) * TILES // (tiles * targets))
    base = -(-largest // 2)
    most = largest - base
    more = jnp.clip(-(-offsets[-1] // targets) - base, 0, most)

    groups = tensor_pattern.shape[0]
    flags = [tensor_pattern.transpose(1, 2, 0).reshape(local_blocks * W, groups)]
    flags.append(green_pattern.reshape(local_blocks * W, 1))
    flags = (jnp.concatenate(flags, axis=1) > 0).astype(jnp.bfloat16)
    lines = -(-local_blocks * W // SUB) * SUB
    flags = jnp.pad(flags, ((0, lines - local_blocks * W), (0, LANES - groups - 1)))
    square = (local_blocks * W * BS, BS)
    packed = jnp.concatenate([green_occ.reshape(square), green_virt.reshape(square)], axis=1)
    packed = gather(jnp.concatenate([packed, flags], axis=0), "orb")

    first, outgoing = send_layout(three_center, offsets, counts, select, base * targets, most * targets)
    packed, first = lax.optimization_barrier((packed, first))
    left = lax.all_to_all(
        first.reshape(targets, base * pieces, SUB, LANES), both, split_axis=0, concat_axis=0, tiled=True
    )

    flags = packed[:, square[0] : square[0] + local_blocks * W, :].reshape(blocks * W, LANES)
    mine = (orb * rows + jnp.arange(pieces * SUB, dtype=jnp.int32)) // ABS
    wanted = mine[:, None] == jnp.arange(LANES, dtype=jnp.int32)[None, :]
    keep = lax.dot_general(
        wanted.astype(flags.dtype),
        jnp.pad(flags, ((0, LANES - blocks * W), (0, 0))),
        (((1,), (1,)), ((), ())),
        preferred_element_type=jnp.float32,
    )
    held_pieces = rows // SUB + (1 if rows % SUB else 0)
    kept = keep[: held_pieces * SUB].astype(jnp.bfloat16).reshape(held_pieces, SUB, LANES)

    diagonal = jnp.arange(W, dtype=jnp.int32) == R
    green_all = flags[:, groups].reshape(blocks, W)
    green_keep = ((green_all > 0) | diagonal[None, :]) & inside
    limits = jnp.stack(
        [jnp.where(green_keep, partner_size, 0), jnp.broadcast_to(atom_size[:, None], (blocks, W))], axis=2
    )
    x = x_layout(
        three_center, offsets, counts, keep[:rows, : blocks * W], limits.reshape(-1), packed, select, largest * targets
    )

    me = aux * n_orb + orb
    slot = jnp.arange(largest * tiles, dtype=jnp.int32) // tiles
    mine = jnp.where(slot < base, me * base + slot, targets * base + me * more + slot - base)[None, :]
    ends = jnp.pad(offsets[1:], (0, LANES - blocks * W))[:, None]
    held = (mine >= jnp.pad(offsets[:-1], (0, LANES - blocks * W))[:, None]) & (mine < ends)

    received = lax.switch(
        more,
        [functools.partial(exchange, base, most, pieces, k) for k in range(most + 1)],
        outgoing,
        x,
        kept,
    )
    held = held.astype(jnp.bfloat16)
    part = chi_part((base + more).reshape(1), left, received, held, rows, n_aux)
    whole = rows // SUB * SUB
    chi = total_part(part, rows)[:rows]
    chi = jnp.concatenate(
        [
            chi[:, : targets * whole].reshape(rows, targets, whole),
            chi[:, targets * whole :].reshape(rows, targets, rows - whole),
        ],
        axis=2,
    )
    return chi.reshape(rows, functions)


def solution(mesh):
    return jax.shard_map(
        body,
        mesh=mesh,
        in_specs=(
            P(("aux", "orb"), None, None, None),
            P(),
            P("aux", "orb", None),
            P("orb", None, None),
            P("orb", None, None),
            P("orb", None),
        ),
        out_specs=P(("aux", "orb"), None),
        check_vma=False,
    )
```

```python
import functools

import jax
import jax.numpy as jnp
import numpy as np
from jax import lax
from jax.experimental import pallas as pl
from jax.experimental.pallas import tpu as pltpu
from jax.sharding import PartitionSpec as P

BS = 64
R = 1
W = 3
ABS = 16
LANES = 128
SUB = 8
TILES = BS * BS // LANES
PER = LANES // BS
GROUP = 16
PARTS = 4


def unit_shape(rows):
    rest = rows % SUB
    tiles = SUB // rest if rest else 1
    return tiles, (rows // SUB) * tiles + (1 if rest else 0)


def gather(x, axis):
    count = 1
    for name in axis if isinstance(axis, tuple) else (axis,):
        count *= lax.axis_size(name)
    return lax.all_to_all(
        jnp.broadcast_to(x[None], (count,) + x.shape), axis, split_axis=0, concat_axis=0, tiled=True
    )


def write_unit(out_ref, unit, rows, load):
    tiles, pieces = unit_shape(rows)
    whole = rows // SUB
    rest = rows % SUB
    for j in range(tiles):
        for q in range(whole):
            out_ref[unit * pieces + j * whole + q] = load(j, q * SUB).astype(out_ref.dtype)
    if rest:
        place = lax.broadcasted_iota(jnp.int32, (SUB, LANES), 0) // rest
        last = load(0, whole * SUB)
        for j in range(1, tiles):
            last = jnp.where(place == j, load(j, whole * SUB - j * rest), last)
        out_ref[unit * pieces + tiles * whole] = last.astype(out_ref.dtype)


def selections():
    counts = range(BS // 2, BS + 1, SUB)
    chosen = np.zeros((len(counts), 2 * GROUP * BS // (4 * LANES), GROUP // 2 * BS, 2 * LANES), np.float32)
    for i, count in enumerate(counts):
        for k in range(chosen.shape[1]):
            start = min(2 * LANES * k // count // PER, GROUP // 4) * PER
            packed = 2 * LANES * k + np.arange(2 * LANES)
            row, column = packed // count, packed % count
            ok = (row < GROUP) & (row < start + GROUP // 2)
            chosen[i, k, ((row - start) * BS + column)[ok], np.arange(2 * LANES)[ok]] = 1
    return jnp.asarray(chosen, jnp.bfloat16)


def pack_block(n, count_ref, select_ref, rows, load, a_ref, c_ref):
    reach = a_ref.shape[0] // (W * BS // GROUP)
    for i in range(W * BS // GROUP):
        for j in range(GROUP // PER):
            a_ref[i * reach : (i + 1) * reach, j * LANES : (j + 1) * LANES] = load(
                i * (GROUP // PER) + j, reach
            ).astype(a_ref.dtype)
    count = count_ref[n]
    which = count // SUB - BS // 2 // SUB

    for k in range(select_ref.shape[1]):
        start = jnp.minimum(LANES * k // count, GROUP // 4)
        at = pl.multiple_of(start * LANES, LANES)
        out = jnp.dot(
            a_ref[:, pl.ds(at, GROUP // 2 * BS)],
            select_ref[which, k],
            preferred_element_type=jnp.float32,
        )
        for h in range(2):
            c_ref[2 * k + h] = out[:, h * LANES : (h + 1) * LANES]


def units_loop(begin, end, unit):
    fours = (end - begin) // 4

    def four(i, carry):
        for k in range(4):
            unit(begin + 4 * i + k)
        return carry

    def one(u, carry):
        unit(u)
        return carry

    lax.fori_loop(0, fours, four, 0)
    lax.fori_loop(begin + 4 * fours, end, one, 0)


def packed_load(n, d, u, tiles, count_ref, c_ref):
    reach = c_ref.shape[1] // (W * BS // GROUP)
    each = count_ref[n] * GROUP // LANES

    def load(j, p):
        tile = u * tiles + j
        group = sum((tile >= g * each).astype(jnp.int32) for g in range(1, BS // GROUP))
        at = (d * (BS // GROUP) + group) * reach + p
        return c_ref[tile - group * each, pl.ds(at, SUB), :]

    return load


def clear_units(out_ref, begin, end, rows):
    _, pieces = unit_shape(rows)
    none = jnp.zeros((SUB, LANES), out_ref.dtype)

    def clear(u, carry):
        for i in range(pieces):
            out_ref[u * pieces + i] = none
        return carry

    lax.fori_loop(begin, jnp.minimum(end, out_ref.shape[0] // pieces), clear, 0)


def send_kernel(spare, offset_ref, count_ref, t_ref, select_ref, base_ref, more_ref, wide_ref, a_ref, c_ref):
    rows, _, blocks, _ = t_ref.shape
    tiles, pieces = unit_shape(rows)
    step = W * TILES * blocks + SUB
    split = base_ref.shape[0] // pieces

    def widen(p, carry):
        for d in range(W):
            x = t_ref[p, d].astype(jnp.float32)
            for i in range(TILES):
                at = pl.multiple_of(p * step + (d * TILES + i) * blocks, SUB)
                wide_ref[pl.ds(at, blocks), :] = x[:, i * LANES : (i + 1) * LANES]
        return carry

    lax.fori_loop(0, rows, widen, 0)

    def block(n, carry):
        def rows_of(i, reach):
            return wide_ref[pl.ds(i * blocks + n, reach, stride=step), :]

        pack_block(n, count_ref, select_ref, rows, rows_of, a_ref, c_ref)
        for d in range(W):
            first = offset_ref[n * W + d]
            count = offset_ref[n * W + d + 1] - first
            turn = jnp.clip(split - first, 0, count)

            def unit(ref, begin, u):
                load = packed_load(n, d, u, tiles, count_ref, c_ref)
                write_unit(ref, first + u - begin, rows, load)

            units_loop(0, turn, functools.partial(unit, base_ref, 0))
            units_loop(turn, count, functools.partial(unit, more_ref, split))
        return carry

    lax.fori_loop(0, blocks, block, 0)
    total = offset_ref[blocks * W]
    clear_units(base_ref, jnp.minimum(total, split), split, rows)
    after = jnp.maximum(total - split, 0)
    clear_units(more_ref, after, after + spare, rows)


def send_layout(three_center, offsets, counts, select, base_units, more_units, spare):
    rows, blocks = three_center.shape[:2]
    _, pieces = unit_shape(rows)
    reach = rows // SUB * SUB + SUB
    return pl.pallas_call(
        functools.partial(send_kernel, spare),
        in_specs=[pl.BlockSpec(memory_space=pltpu.SMEM)] * 2
        + [pl.BlockSpec(memory_space=pltpu.VMEM)] * 2,
        out_specs=[pl.BlockSpec(memory_space=pltpu.VMEM)] * 2,
        out_shape=[
            jax.ShapeDtypeStruct((units * pieces, SUB, LANES), jnp.bfloat16)
            for units in (base_units, more_units)
        ],
        scratch_shapes=[
            pltpu.VMEM((reach * (W * TILES * blocks + SUB), LANES), jnp.float32),
            pltpu.VMEM((W * BS // GROUP * reach, GROUP * BS), jnp.bfloat16),
            pltpu.VMEM((GROUP // PER, W * BS // GROUP * reach, LANES), jnp.float32),
        ],
        compiler_params=pltpu.CompilerParams(vmem_limit_bytes=48 << 20),
        cost_estimate=pl.CostEstimate(
            flops=0, bytes_accessed=three_center.size * 16, transcendentals=0
        ),
    )(offsets, counts, three_center.transpose(0, 2, 1, 3), select)


def green_factors(limit_ref, green_ref, blocks, gm_ref, z_ref, v_ref, o_ref):
    local = blocks // green_ref.shape[0]
    row = lax.broadcasted_iota(jnp.int32, (BS, LANES), 0)
    lane = lax.broadcasted_iota(jnp.int32, (BS, LANES), 1)
    for b in range(blocks * W):
        n, d = b // W, b % W
        at = (n % local * W + d) * BS
        g = green_ref[n // local, at : at + BS, :].astype(jnp.float32)
        g = jnp.where((row < limit_ref[2 * b]) & (lane % BS < limit_ref[2 * b + 1]), g, 0.0)
        gm_ref[b * BS : (b + 1) * BS, :] = g.astype(gm_ref.dtype)
        left = jnp.where(lane < BS, pltpu.roll(g, BS, 1), 0.0).astype(v_ref.dtype)
        right = jnp.where(lane >= BS, g, 0.0).astype(v_ref.dtype)
        v_ref[b, :BS, :LANES] = left
        v_ref[b, :BS, LANES:] = right
        v_ref[b, BS:, :LANES] = right
        v_ref[b, BS:, LANES:] = left
    pick = (lane == row % TILES * PER + row // TILES).astype(gm_ref.dtype)
    turned = lax.dot_general(
        pick, gm_ref[...], (((1,), (1,)), ((), ())), preferred_element_type=jnp.float32
    ).astype(gm_ref.dtype)
    pairs = blocks * W // PER
    stacked = jnp.concatenate([turned[:, c * LANES : (c + 1) * LANES] for c in range(pairs)], axis=0)
    into = lax.broadcasted_iota(jnp.int32, (LANES, LANES), 1)
    source = into // BS * BS + into % TILES * PER + into % BS // TILES
    perm = (lax.broadcasted_iota(jnp.int32, (LANES, LANES), 0) == source).astype(gm_ref.dtype)
    z_ref[...] = jnp.dot(stacked, perm, preferred_element_type=jnp.float32).astype(z_ref.dtype)
    o_ref[...] = jnp.zeros(o_ref.shape, o_ref.dtype)
    for n in range(blocks):
        for p in range(PER):
            for d in range(W):
                m = n + d - R
                if m < 0 or m >= blocks:
                    continue
                to = (p * W + d) * TILES
                for h in range(PER):
                    for e in range(W):
                        if abs(e - d) <= R:
                            b = m * W + e - d + R
                            line = b // PER * BS + p * TILES
                            at = b % PER * BS + (p + h) % PER * TILES
                            col = (h * W + e) * TILES
                            o_ref[n, to : to + TILES, col : col + TILES] = z_ref[
                                line : line + TILES, at : at + TILES
                            ]


def x_kernel(
    base_units, spare, offset_ref, count_ref, keep_ref, limit_ref, t_ref, green_ref, select_ref, out_ref,
    wide_ref, t2_ref, second_ref, x_ref, gm_ref, z_ref, v_ref, o_ref, a_ref, c_ref,
):
    rows, _, blocks, _ = t_ref.shape
    tiles, _ = unit_shape(rows)
    depth = W * TILES
    green_factors(limit_ref, green_ref, blocks, gm_ref, z_ref, v_ref, o_ref)

    def turn(p, carry):
        for d in range(W):
            x = t_ref[p, d].astype(jnp.float32)
            for i in range(TILES):
                wide_ref[i * blocks : (i + 1) * blocks, :] = x[:, i * LANES : (i + 1) * LANES]
            for n in range(blocks):
                kept = wide_ref[pl.ds(n, TILES, stride=blocks), :] * keep_ref[p, n * W + d]
                at = pl.multiple_of(p * TILES, TILES)
                t2_ref[n * W + d, pl.ds(at, TILES), :] = kept.astype(t2_ref.dtype)
        return carry

    lax.fori_loop(0, rows, turn, 0)
    lane = lax.broadcasted_iota(jnp.int32, (1, LANES), 1)

    def block(n, carry):
        for e in range(W):
            total = None
            for d in range(W):
                if abs(e - d) <= R:
                    m = jnp.clip(n + d - R, 0, blocks - 1)
                    part = jnp.dot(
                        t2_ref[m * W + e - d + R], v_ref[n * W + d], preferred_element_type=jnp.float32
                    )
                    total = part if total is None else total + part
            total = total.astype(second_ref.dtype)
            for p in range(rows):
                for h in range(PER):
                    at = h * depth + e * TILES
                    second_ref[at : at + TILES, p * LANES : (p + 1) * LANES] = total[
                        p * TILES : (p + 1) * TILES, h * LANES : (h + 1) * LANES
                    ]
        chunk = 5 if rows % 5 == 0 else 1
        for c in range(rows // chunk):
            both = jnp.dot(
                o_ref[n],
                second_ref[:, c * chunk * LANES : (c + 1) * chunk * LANES],
                preferred_element_type=jnp.float32,
            )
            for i in range(chunk):
                p = c * chunk + i
                at = slice(i * LANES, (i + 1) * LANES)
                x_ref[p * (depth + 1) : p * (depth + 1) + depth, :] = jnp.where(
                    lane < BS, both[:depth, at], both[depth:, at]
                )
        def rows_of(i, reach):
            return x_ref[pl.ds(i, reach, stride=depth + 1), :]

        pack_block(n, count_ref, select_ref, rows, rows_of, a_ref, c_ref)
        for d in range(W):
            first = offset_ref[n * W + d]

            def unit(u):
                load = packed_load(n, d, u, tiles, count_ref, c_ref)
                write_unit(out_ref, first + u, rows, load)

            units_loop(0, offset_ref[n * W + d + 1] - first, unit)
        return carry

    lax.fori_loop(0, blocks, block, 0)
    total = offset_ref[blocks * W]
    clear_units(out_ref, total, jnp.maximum(total + spare, base_units), rows)


def x_layout(three_center, offsets, counts, keep, limits, green, select, units, base_units, spare):
    rows, blocks = three_center.shape[:2]
    _, pieces = unit_shape(rows)
    depth = W * TILES
    reach = rows // SUB * SUB + SUB
    return pl.pallas_call(
        functools.partial(x_kernel, base_units, spare),
        in_specs=[pl.BlockSpec(memory_space=pltpu.SMEM)] * 4
        + [pl.BlockSpec(memory_space=pltpu.VMEM)] * 3,
        out_specs=pl.BlockSpec(memory_space=pltpu.VMEM),
        out_shape=jax.ShapeDtypeStruct((units * pieces, SUB, LANES), jnp.bfloat16),
        scratch_shapes=[
            pltpu.VMEM((TILES * blocks, LANES), jnp.float32),
            pltpu.VMEM((blocks * W, rows * TILES, LANES), jnp.bfloat16),
            pltpu.VMEM((PER * depth, rows * LANES), jnp.bfloat16),
            pltpu.VMEM((reach * (depth + 1), LANES), jnp.float32),
            pltpu.VMEM((blocks * W * BS, LANES), jnp.bfloat16),
            pltpu.VMEM((blocks * W // PER * BS, LANES), jnp.bfloat16),
            pltpu.VMEM((blocks * W, LANES, PER * LANES), jnp.bfloat16),
            pltpu.VMEM((blocks, PER * depth, PER * depth), jnp.bfloat16),
            pltpu.VMEM((W * BS // GROUP * reach, GROUP * BS), jnp.bfloat16),
            pltpu.VMEM((GROUP // PER, W * BS // GROUP * reach, LANES), jnp.float32),
        ],
        compiler_params=pltpu.CompilerParams(vmem_limit_bytes=48 << 20),
        cost_estimate=pl.CostEstimate(
            flops=blocks * rows * (7 * TILES * LANES * LANES * 4 + 16 * TILES * TILES * 9 * LANES),
            bytes_accessed=three_center.size * 8,
            transcendentals=0,
        ),
    )(offsets, counts, keep, limits, three_center.transpose(0, 2, 1, 3), green, select)


def more_units(total, t):
    turn = t % PARTS
    return t // PARTS * total + sum((total + r) // PARTS * (turn > r) for r in range(PARTS)), (total + turn) // PARTS


def exchange_kernel(base, total, most, pieces, more_ref, x_ref, keep_ref, out_ref, send_sem, recv_sem, own_sem):
    n_aux, n_orb = lax.axis_size("aux"), lax.axis_size("orb")
    targets = n_aux * n_orb
    aux, orb = lax.axis_index("aux"), lax.axis_index("orb")
    me = aux * n_orb + orb
    few, step = total // PARTS, PARTS - total % PARTS

    def spans(t, source, more):
        yield keep_ref, out_ref.at[source, pl.ds((2 * most + base) * pieces, keep_ref.shape[0])]
        size = base * pieces
        yield x_ref.at[pl.ds(t * size, size)], out_ref.at[source, pl.ds(most * pieces, size)]
        if more:
            size = more * pieces
            at, _ = more_units(total, t)
            yield (
                x_ref.at[pl.ds((targets * base + at) * pieces, size)],
                out_ref.at[source, pl.ds((most + base) * pieces, size)],
            )
            yield more_ref.at[pl.ds(at * pieces, size)], out_ref.at[source, pl.ds(0, size)]

    def by_size(t, act):
        if step == PARTS:
            act(few)
        else:
            pl.when(t % PARTS < step)(functools.partial(act, few))
            pl.when(t % PARTS >= step)(functools.partial(act, few + 1))

    def partner(i):
        return lax.rem(aux + lax.rem(i, n_aux), n_aux), lax.rem(orb + i // n_aux + n_orb // 2, n_orb)

    def copies(t, source, to, more):
        return [
            pltpu.make_async_remote_copy(
                src_ref=src,
                dst_ref=dst,
                send_sem=send_sem.at[k, t],
                recv_sem=recv_sem.at[k, source],
                device_id=to,
                device_id_type=pl.DeviceIdType.MESH,
            )
            for k, (src, dst) in enumerate(spans(t, source, more))
        ]

    def start(i, carry):
        to = partner(i)
        t = to[0] * n_orb + to[1]

        def act(more):
            for copy in copies(t, me, to, more):
                copy.start()

        pl.when(t != me)(lambda: by_size(t, act))
        return carry

    lax.fori_loop(0, targets, start, 0)

    def own(finish, more):
        for k, (src, dst) in enumerate(spans(me, me, more)):
            copy = pltpu.make_async_copy(src, dst, own_sem.at[k])
            copy.wait() if finish else copy.start()

    by_size(me, functools.partial(own, False))

    def finish(i, carry):
        to = partner(i)
        t = to[0] * n_orb + to[1]

        def received(more):
            for copy in copies(me, t, to, more):
                copy.wait_recv()

        def sent(more):
            for copy in copies(t, me, to, more):
                copy.wait_send()

        def both():
            by_size(me, received)
            by_size(t, sent)

        pl.when(t != me)(both)
        return carry

    lax.fori_loop(0, targets, finish, 0)
    by_size(me, functools.partial(own, True))


def exchange(base, most, pieces, total, outgoing, x, keep):
    targets = lax.axis_size("aux") * lax.axis_size("orb")
    return pl.pallas_call(
        functools.partial(exchange_kernel, base, total, most, pieces),
        in_specs=[pl.BlockSpec(memory_space=pl.ANY)] * 3,
        out_specs=pl.BlockSpec(memory_space=pl.ANY),
        out_shape=jax.ShapeDtypeStruct(
            (targets, (2 * most + base) * pieces + keep.shape[0], SUB, LANES), jnp.bfloat16
        ),
        scratch_shapes=[
            pltpu.SemaphoreType.DMA((4, targets)),
            pltpu.SemaphoreType.DMA((4, targets)),
            pltpu.SemaphoreType.DMA((4,)),
        ],
        compiler_params=pltpu.CompilerParams(has_side_effects=True),
    )(outgoing, x, keep)


def chi_kernel(rows, share_ref, left_ref, both_ref, held_ref, out_ref, l_ref, r_ref, k_ref):
    sources = left_ref.shape[0]
    tiles, pieces = unit_shape(rows)
    base = left_ref.shape[1] // pieces
    most = (both_ref.shape[1] // pieces - base) // 2
    whole, rest = rows // SUB, rows % SUB
    main = sources * whole * SUB

    def assemble(from_ref, first, to_ref, u, tiles=tiles):
        for j in range(tiles):
            at = slice((u * tiles + j) * LANES, (u * tiles + j + 1) * LANES)
            for s in range(sources):
                if whole:
                    i = first + j * whole
                    to_ref[s * whole * SUB : (s + 1) * whole * SUB, at] = jnp.concatenate(
                        [from_ref[s, i + q] for q in range(whole)], axis=0
                    )
            if rest:
                i = first + tiles * whole
                step = SUB // rest
                for s in range(0, sources, step):
                    to_ref[main + s * rest : main + (s + step) * rest, at] = jnp.concatenate(
                        [from_ref[s + t, i, j * rest : (j + 1) * rest, :] for t in range(step)],
                        axis=0,
                    )

    assemble(both_ref, (2 * most + base) * pieces, k_ref, 0, 1)
    keep = jnp.dot(k_ref[...], held_ref[...], preferred_element_type=jnp.float32)
    keep = keep.astype(l_ref.dtype)

    def fill(u):
        if u < base:
            assemble(left_ref, u * pieces, l_ref, u)
        else:
            assemble(both_ref, (u - base) * pieces, l_ref, u)
        assemble(both_ref, (most + u) * pieces, r_ref, u)
        for i in range(u * tiles, (u + 1) * tiles):
            at = slice(i * LANES, (i + 1) * LANES)
            l_ref[:, at] = l_ref[:, at] * keep[:, i : i + 1]

    def clear(u):
        at = slice(u * tiles * LANES, (u + 1) * tiles * LANES)
        l_ref[:, at] = jnp.zeros((l_ref.shape[0], tiles * LANES), l_ref.dtype)
        r_ref[:, at] = jnp.zeros((r_ref.shape[0], tiles * LANES), r_ref.dtype)

    for u in range(base + most):
        if u < base:
            fill(u)
        else:
            pl.when(u < share_ref[0])(functools.partial(fill, u))
            pl.when(u >= share_ref[0])(functools.partial(clear, u))
    chi = lax.dot_general(
        l_ref[...], r_ref[...], (((1,), (1,)), ((), ())), preferred_element_type=jnp.float32
    ).astype(out_ref.dtype)
    groups, height = out_ref.shape[:2]
    top = main // groups
    for a in range(groups):
        out_ref[a, :top, :] = chi[a * top : (a + 1) * top]
        if rest:
            low = height - top
            out_ref[a, top:, :] = chi[main + a * low : main + (a + 1) * low]


def chi_part(share, left, both, held, rows, groups):
    sources = left.shape[0]
    tiles, pieces = unit_shape(rows)
    functions = sources * rows
    units = (left.shape[1] // pieces + both.shape[1] // pieces) // 2
    depth = units * tiles * LANES
    return pl.pallas_call(
        functools.partial(chi_kernel, rows),
        in_specs=[pl.BlockSpec(memory_space=pltpu.SMEM)]
        + [pl.BlockSpec(memory_space=pltpu.VMEM)] * 3,
        out_specs=pl.BlockSpec(memory_space=pltpu.VMEM),
        out_shape=jax.ShapeDtypeStruct((groups, functions // groups, functions), jnp.float32),
        scratch_shapes=[pltpu.VMEM((functions, k), jnp.bfloat16) for k in (depth, depth, LANES)],
        compiler_params=pltpu.CompilerParams(vmem_limit_bytes=36 << 20),
    )(share, left, both, held)


def total_kernel(rows, cores, chunks, part_ref, out_ref, pair_ref, left_ref, near_ref, held_ref, right_ref, far_ref, *sems):
    n_aux, n_orb = lax.axis_size("aux"), lax.axis_size("orb")
    aux, orb = lax.axis_index("aux"), lax.axis_index("orb")
    chips = n_aux // cores
    chip, core = aux // cores, lax.rem(aux, cores)
    other = cores - 1 - core
    whole, rest = rows // SUB * SUB, rows % SUB
    pair_send, pair_recv, near_send, near_recv, far_send, far_recv = sems

    def remote(src, dst, send, recv, to):
        return pltpu.make_async_remote_copy(
            src_ref=src, dst_ref=dst, send_sem=send, recv_sem=recv,
            device_id=to, device_id_type=pl.DeviceIdType.MESH,
        )

    def pair(c, i):
        to = lax.rem(chip + i, chips)
        at = chunks[c]
        return remote(
            part_ref.at[to * cores + other, :, at], pair_ref.at[to, :, at],
            pair_send.at[c, i], pair_recv.at[c, i], (chip * cores + other, orb),
        )

    def near(c, i):
        at = chunks[c]
        return remote(
            left_ref.at[i, :, at], near_ref.at[i, :, at],
            near_send.at[c, i], near_recv.at[c, i], (lax.rem(chip + i, chips) * cores + core, orb),
        )

    def far(c, i):
        to = lax.rem(orb + i, n_orb)
        at = chunks[c]
        return remote(
            right_ref.at[to, :, at], far_ref.at[i, :, at], far_send.at[c, i], far_recv.at[c, i], (aux, to)
        )

    order = list(range(1, chips)) + [0]
    for c in range(len(chunks)):
        for i in order:
            pair(c, i).start()
    for c, at in enumerate(chunks):
        for i in order:
            to = lax.rem(chip + i, chips)
            pair(c, i).wait_recv()
            both = part_ref[to * cores + core, :, at] + pair_ref[to, :, at]
            if i:
                left_ref[i, :, at] = both.astype(left_ref.dtype)
                near(c, i).start()
            else:
                held_ref[:, at] = both
    for c, at in enumerate(chunks):
        total = held_ref[:, at]
        for i in range(1, chips):
            near(c, i).wait_recv()
            total = total + near_ref[i, :, at].astype(jnp.float32)
        held_ref[:, at] = total
        for o in range(n_orb):
            right_ref[o, :whole, at] = total[o * whole : (o + 1) * whole].astype(right_ref.dtype)
            if rest:
                low = n_orb * whole + o * rest
                tail = total[low // SUB * SUB : low // SUB * SUB + SUB]
                if low % SUB:
                    tail = pltpu.roll(tail, SUB - low % SUB, 0)
                right_ref[o, whole:, at] = tail.astype(right_ref.dtype)
        for i in range(1, n_orb):
            far(c, i).start()
    for c, at in enumerate(chunks):
        total = right_ref[orb, :, at].astype(jnp.float32)
        for i in range(1, n_orb):
            far(c, i).wait_recv()
            total = total + far_ref[i, :, at].astype(jnp.float32)
        out_ref[:, at] = total
    for c in range(len(chunks)):
        for i in range(chips):
            pair(c, i).wait_send()
        for i in range(1, chips):
            near(c, i).wait_send()
        for i in range(1, n_orb):
            far(c, i).wait_send()


def total_part(part, rows):
    n_aux, height, functions = part.shape
    n_orb = lax.axis_size("orb")
    cores = 2
    chips = n_aux // cores
    tall = -(-rows // SUB) * SUB
    cut = functions // LANES // 2 * LANES
    chunks = (slice(0, cut), slice(cut, functions))
    wide = jnp.float32
    return pl.pallas_call(
        functools.partial(total_kernel, rows, cores, chunks),
        in_specs=[pl.BlockSpec(memory_space=pltpu.VMEM)],
        out_specs=pl.BlockSpec(memory_space=pltpu.VMEM),
        out_shape=jax.ShapeDtypeStruct((tall, functions), wide),
        scratch_shapes=[
            pltpu.VMEM((chips, height, functions), wide),
            pltpu.VMEM((chips, height, functions), jnp.bfloat16),
            pltpu.VMEM((chips, height, functions), jnp.bfloat16),
            pltpu.VMEM((height, functions), wide),
            pltpu.VMEM((n_orb, tall, functions), jnp.bfloat16),
            pltpu.VMEM((n_orb, tall, functions), jnp.bfloat16),
        ]
        + [pltpu.SemaphoreType.DMA((2, k)) for k in (chips, chips, chips, chips, n_orb, n_orb)],
        compiler_params=pltpu.CompilerParams(has_side_effects=True, vmem_limit_bytes=36 << 20),
    )(part)


def body(three_center, atom_size, tensor_pattern, green_occ, green_virt, green_pattern):
    both = ("aux", "orb")
    n_aux, n_orb = lax.axis_size("aux"), lax.axis_size("orb")
    aux, orb = lax.axis_index("aux"), lax.axis_index("orb")
    rows, blocks = three_center.shape[0], three_center.shape[1]
    local_blocks = green_occ.shape[0]
    area = BS * BS
    targets = n_aux * n_orb
    functions = targets * rows
    tiles, pieces = unit_shape(rows)

    owned = jnp.arange(blocks, dtype=jnp.int32)[:, None]
    partner = owned + jnp.arange(W, dtype=jnp.int32)[None, :] - R
    inside = (partner >= 0) & (partner < blocks)
    catalog = jnp.arange(blocks, dtype=jnp.int32)
    partner_size = jnp.sum(jnp.where(partner[:, :, None] == catalog, atom_size, 0), axis=2)
    counts = jnp.clip(-(-atom_size // SUB) * SUB, BS // 2, BS)
    taken = -(-partner_size * counts[:, None] // (tiles * LANES)) * inside
    select = selections()
    before = jnp.arange(blocks * W + 1, dtype=jnp.int32)[:, None]
    before = before > jnp.arange(blocks * W, dtype=jnp.int32)[None, :]
    offsets = jnp.sum(jnp.where(before, taken.reshape(1, -1), 0), axis=1).astype(jnp.int32)
    largest = -(-(blocks * W - 2 * R) * TILES // (tiles * targets))
    base = -(-largest // 2)
    most = largest - base
    total = jnp.clip(-(-offsets[-1] * PARTS // targets) - base * PARTS, 0, most * PARTS)
    me = aux * n_orb + orb
    ahead, more = more_units(total, me)

    groups = tensor_pattern.shape[0]
    flags = [tensor_pattern.transpose(1, 2, 0).reshape(local_blocks * W, groups)]
    flags.append(green_pattern.reshape(local_blocks * W, 1))
    flags = (jnp.concatenate(flags, axis=1) > 0).astype(jnp.bfloat16)
    own = local_blocks * W
    flags = jnp.pad(flags, ((0, 0), (0, LANES - groups - 1))).reshape(-1)
    lines = -(-own * LANES // (BS * BS))
    flags = jnp.pad(flags, (0, lines * BS * BS - own * LANES)).reshape(lines, BS * BS)
    packed = [green_occ.reshape(own, BS * BS), green_virt.reshape(own, BS * BS), flags]
    packed = gather(jnp.concatenate(packed, axis=0), "orb")

    first, outgoing = send_layout(three_center, offsets, counts, select, base * targets, most * targets, targets // PARTS)
    packed, _ = lax.optimization_barrier((packed, first))
    left = lax.all_to_all(
        first.reshape(targets, base * pieces, SUB, LANES), both, split_axis=0, concat_axis=0, tiled=True
    )

    flags = packed[:, 2 * own :].reshape(n_orb, -1)[:, : own * LANES].reshape(blocks * W, LANES)
    green = jnp.concatenate(
        [packed[:, i * own : (i + 1) * own].reshape(n_orb, own * BS, BS) for i in range(2)], axis=2
    )
    mine = (orb * rows + jnp.arange(pieces * SUB, dtype=jnp.int32)) // ABS
    wanted = mine[:, None] == jnp.arange(LANES, dtype=jnp.int32)[None, :]
    keep = lax.dot_general(
        wanted.astype(flags.dtype),
        jnp.pad(flags, ((0, LANES - blocks * W), (0, 0))),
        (((1,), (1,)), ((), ())),
        preferred_element_type=jnp.float32,
    )
    held_pieces = rows // SUB + (1 if rows % SUB else 0)
    kept = keep[: held_pieces * SUB].astype(jnp.bfloat16).reshape(held_pieces, SUB, LANES)

    diagonal = jnp.arange(W, dtype=jnp.int32) == R
    green_all = flags[:, groups].reshape(blocks, W)
    green_keep = ((green_all > 0) | diagonal[None, :]) & inside
    limits = jnp.stack(
        [jnp.where(green_keep, partner_size, 0), jnp.broadcast_to(atom_size[:, None], (blocks, W))], axis=2
    )
    x = x_layout(
        three_center, offsets, counts, keep[:rows, : blocks * W], limits.reshape(-1), green, select,
        largest * targets, base * targets, targets // PARTS,
    )

    slot = jnp.arange(largest * tiles, dtype=jnp.int32) // tiles
    mine = jnp.where(slot < base, me * base + slot, targets * base + ahead + slot - base)[None, :]
    ends = jnp.pad(offsets[1:], (0, LANES - blocks * W))[:, None]
    held = (mine >= jnp.pad(offsets[:-1], (0, LANES - blocks * W))[:, None]) & (mine < ends)

    received = lax.switch(
        total,
        [functools.partial(exchange, base, most, pieces, k) for k in range(most * PARTS + 1)],
        outgoing,
        x,
        kept,
    )
    held = held.astype(jnp.bfloat16)
    part = chi_part((base + more).reshape(1), left, received, held, rows, n_aux)
    whole = rows // SUB * SUB
    chi = total_part(part, rows)[:rows]
    chi = jnp.concatenate(
        [
            chi[:, : targets * whole].reshape(rows, targets, whole),
            chi[:, targets * whole :].reshape(rows, targets, rows - whole),
        ],
        axis=2,
    )
    return chi.reshape(rows, functions)


def solution(mesh):
    return jax.shard_map(
        body,
        mesh=mesh,
        in_specs=(
            P(("aux", "orb"), None, None, None),
            P(),
            P("aux", "orb", None),
            P("orb", None, None),
            P("orb", None, None),
            P("orb", None),
        ),
        out_specs=P(("aux", "orb"), None),
        check_vma=False,
    )
```

```python
import functools

import jax
import jax.numpy as jnp
import numpy as np
from jax import lax
from jax.experimental import pallas as pl
from jax.experimental.pallas import tpu as pltpu
from jax.sharding import PartitionSpec as P

BS = 64
R = 1
W = 3
ABS = 16
LANES = 128
SUB = 8
TILES = BS * BS // LANES
PER = LANES // BS
GROUP = 16
PARTS = 4


def unit_shape(rows):
    rest = rows % SUB
    tiles = SUB // rest if rest else 1
    return tiles, (rows // SUB) * tiles + (1 if rest else 0)


def gather(x, axis):
    count = 1
    for name in axis if isinstance(axis, tuple) else (axis,):
        count *= lax.axis_size(name)
    return lax.all_to_all(
        jnp.broadcast_to(x[None], (count,) + x.shape), axis, split_axis=0, concat_axis=0, tiled=True
    )


def write_unit(out_ref, unit, rows, load):
    tiles, pieces = unit_shape(rows)
    whole = rows // SUB
    rest = rows % SUB
    for j in range(tiles):
        for q in range(whole):
            out_ref[unit * pieces + j * whole + q] = load(j, q * SUB).astype(out_ref.dtype)
    if rest:
        place = lax.broadcasted_iota(jnp.int32, (SUB, LANES), 0) // rest
        last = load(0, whole * SUB)
        for j in range(1, tiles):
            last = jnp.where(place == j, load(j, whole * SUB - j * rest), last)
        out_ref[unit * pieces + tiles * whole] = last.astype(out_ref.dtype)


def selections():
    counts = range(BS // 2, BS + 1, SUB)
    chosen = np.zeros((len(counts), 2 * GROUP * BS // (4 * LANES), GROUP // 2 * BS, 2 * LANES), np.float32)
    for i, count in enumerate(counts):
        for k in range(chosen.shape[1]):
            start = min(2 * LANES * k // count // PER, GROUP // 4) * PER
            packed = 2 * LANES * k + np.arange(2 * LANES)
            row, column = packed // count, packed % count
            ok = (row < GROUP) & (row < start + GROUP // 2)
            chosen[i, k, ((row - start) * BS + column)[ok], np.arange(2 * LANES)[ok]] = 1
    return jnp.asarray(chosen, jnp.bfloat16)


def pack_block(n, count_ref, select_ref, rows, load, a_ref, c_ref):
    reach = a_ref.shape[0] // (W * BS // GROUP)
    for i in range(W * BS // GROUP):
        for j in range(GROUP // PER):
            a_ref[i * reach : (i + 1) * reach, j * LANES : (j + 1) * LANES] = load(
                i * (GROUP // PER) + j, reach
            ).astype(a_ref.dtype)
    count = count_ref[n]
    which = count // SUB - BS // 2 // SUB

    for k in range(select_ref.shape[1]):
        start = jnp.minimum(LANES * k // count, GROUP // 4)
        at = pl.multiple_of(start * LANES, LANES)
        out = jnp.dot(
            a_ref[:, pl.ds(at, GROUP // 2 * BS)],
            select_ref[which, k],
            preferred_element_type=jnp.float32,
        )
        for h in range(2):
            c_ref[2 * k + h] = out[:, h * LANES : (h + 1) * LANES]


def units_loop(begin, end, unit):
    fours = (end - begin) // 4

    def four(i, carry):
        for k in range(4):
            unit(begin + 4 * i + k)
        return carry

    def one(u, carry):
        unit(u)
        return carry

    lax.fori_loop(0, fours, four, 0)
    lax.fori_loop(begin + 4 * fours, end, one, 0)


def packed_load(n, d, u, tiles, count_ref, c_ref):
    reach = c_ref.shape[1] // (W * BS // GROUP)
    each = count_ref[n] * GROUP // LANES

    def load(j, p):
        tile = u * tiles + j
        group = sum((tile >= g * each).astype(jnp.int32) for g in range(1, BS // GROUP))
        at = (d * (BS // GROUP) + group) * reach + p
        return c_ref[tile - group * each, pl.ds(at, SUB), :]

    return load


def clear_units(out_ref, begin, end, rows):
    _, pieces = unit_shape(rows)
    none = jnp.zeros((SUB, LANES), out_ref.dtype)

    def clear(u, carry):
        for i in range(pieces):
            out_ref[u * pieces + i] = none
        return carry

    lax.fori_loop(begin, jnp.minimum(end, out_ref.shape[0] // pieces), clear, 0)


def send_kernel(spare, offset_ref, count_ref, t_ref, select_ref, base_ref, more_ref, wide_ref, a_ref, c_ref):
    rows, _, blocks, _ = t_ref.shape
    tiles, pieces = unit_shape(rows)
    step = W * TILES * blocks + SUB
    split = base_ref.shape[0] // pieces

    def widen(p, carry):
        for d in range(W):
            x = t_ref[p, d].astype(jnp.float32)
            for i in range(TILES):
                at = pl.multiple_of(p * step + (d * TILES + i) * blocks, SUB)
                wide_ref[pl.ds(at, blocks), :] = x[:, i * LANES : (i + 1) * LANES]
        return carry

    lax.fori_loop(0, rows, widen, 0)

    def block(n, carry):
        def rows_of(i, reach):
            return wide_ref[pl.ds(i * blocks + n, reach, stride=step), :]

        pack_block(n, count_ref, select_ref, rows, rows_of, a_ref, c_ref)
        for d in range(W):
            first = offset_ref[n * W + d]
            count = offset_ref[n * W + d + 1] - first
            turn = jnp.clip(split - first, 0, count)

            def unit(ref, begin, u):
                load = packed_load(n, d, u, tiles, count_ref, c_ref)
                write_unit(ref, first + u - begin, rows, load)

            units_loop(0, turn, functools.partial(unit, base_ref, 0))
            units_loop(turn, count, functools.partial(unit, more_ref, split))
        return carry

    lax.fori_loop(0, blocks, block, 0)
    total = offset_ref[blocks * W]
    clear_units(base_ref, jnp.minimum(total, split), split, rows)
    after = jnp.maximum(total - split, 0)
    clear_units(more_ref, after, after + spare, rows)


def send_layout(three_center, offsets, counts, select, base_units, more_units, spare):
    rows, blocks = three_center.shape[:2]
    _, pieces = unit_shape(rows)
    reach = rows // SUB * SUB + SUB
    return pl.pallas_call(
        functools.partial(send_kernel, spare),
        in_specs=[pl.BlockSpec(memory_space=pltpu.SMEM)] * 2
        + [pl.BlockSpec(memory_space=pltpu.VMEM)] * 2,
        out_specs=[pl.BlockSpec(memory_space=pltpu.VMEM)] * 2,
        out_shape=[
            jax.ShapeDtypeStruct((units * pieces, SUB, LANES), jnp.bfloat16)
            for units in (base_units, more_units)
        ],
        scratch_shapes=[
            pltpu.VMEM((reach * (W * TILES * blocks + SUB), LANES), jnp.float32),
            pltpu.VMEM((W * BS // GROUP * reach, GROUP * BS), jnp.bfloat16),
            pltpu.VMEM((GROUP // PER, W * BS // GROUP * reach, LANES), jnp.float32),
        ],
        compiler_params=pltpu.CompilerParams(vmem_limit_bytes=56 << 20),
        cost_estimate=pl.CostEstimate(
            flops=0, bytes_accessed=three_center.size * 16, transcendentals=0
        ),
    )(offsets, counts, three_center.transpose(0, 2, 1, 3), select)


def green_factors(limit_ref, green_ref, blocks, gm_ref, z_ref, v_ref, o_ref):
    local = blocks // green_ref.shape[0]
    row = lax.broadcasted_iota(jnp.int32, (BS, LANES), 0)
    lane = lax.broadcasted_iota(jnp.int32, (BS, LANES), 1)
    for b in range(blocks * W):
        n, d = b // W, b % W
        at = (n % local * W + d) * BS
        g = green_ref[n // local, at : at + BS, :].astype(jnp.float32)
        g = jnp.where((row < limit_ref[2 * b]) & (lane % BS < limit_ref[2 * b + 1]), g, 0.0)
        gm_ref[b * BS : (b + 1) * BS, :] = g.astype(gm_ref.dtype)
        left = jnp.where(lane < BS, pltpu.roll(g, BS, 1), 0.0).astype(v_ref.dtype)
        right = jnp.where(lane >= BS, g, 0.0).astype(v_ref.dtype)
        v_ref[b, :BS, :LANES] = left
        v_ref[b, :BS, LANES:] = right
        v_ref[b, BS:, :LANES] = right
        v_ref[b, BS:, LANES:] = left
    pick = (lane == row % TILES * PER + row // TILES).astype(gm_ref.dtype)
    turned = lax.dot_general(
        pick, gm_ref[...], (((1,), (1,)), ((), ())), preferred_element_type=jnp.float32
    ).astype(gm_ref.dtype)
    pairs = blocks * W // PER
    stacked = jnp.concatenate([turned[:, c * LANES : (c + 1) * LANES] for c in range(pairs)], axis=0)
    into = lax.broadcasted_iota(jnp.int32, (LANES, LANES), 1)
    source = into // BS * BS + into % TILES * PER + into % BS // TILES
    perm = (lax.broadcasted_iota(jnp.int32, (LANES, LANES), 0) == source).astype(gm_ref.dtype)
    z_ref[...] = jnp.dot(stacked, perm, preferred_element_type=jnp.float32).astype(z_ref.dtype)
    o_ref[...] = jnp.zeros(o_ref.shape, o_ref.dtype)
    for n in range(blocks):
        for p in range(PER):
            for d in range(W):
                m = n + d - R
                if m < 0 or m >= blocks:
                    continue
                to = (p * W + d) * TILES
                for h in range(PER):
                    for e in range(W):
                        if abs(e - d) <= R:
                            b = m * W + e - d + R
                            line = b // PER * BS + p * TILES
                            at = b % PER * BS + (p + h) % PER * TILES
                            col = (h * W + e) * TILES
                            o_ref[n, to : to + TILES, col : col + TILES] = z_ref[
                                line : line + TILES, at : at + TILES
                            ]


def x_kernel(
    base_units, spare, offset_ref, count_ref, keep_ref, limit_ref, t_ref, green_ref, select_ref, out_ref,
    wide_ref, t2_ref, second_ref, x_ref, gm_ref, z_ref, v_ref, o_ref, a_ref, c_ref,
):
    rows, _, blocks, _ = t_ref.shape
    tiles, _ = unit_shape(rows)
    depth = W * TILES
    green_factors(limit_ref, green_ref, blocks, gm_ref, z_ref, v_ref, o_ref)

    def turn(p, carry):
        for d in range(W):
            x = t_ref[p, d].astype(jnp.float32)
            for i in range(TILES):
                wide_ref[i * blocks : (i + 1) * blocks, :] = x[:, i * LANES : (i + 1) * LANES]
            for n in range(blocks):
                kept = wide_ref[pl.ds(n, TILES, stride=blocks), :] * keep_ref[p, n * W + d]
                at = pl.multiple_of(p * TILES, TILES)
                t2_ref[n * W + d, pl.ds(at, TILES), :] = kept.astype(t2_ref.dtype)
        return carry

    lax.fori_loop(0, rows, turn, 0)
    lane = lax.broadcasted_iota(jnp.int32, (1, LANES), 1)

    def block(n, carry):
        for e in range(W):
            total = None
            for d in range(W):
                if abs(e - d) <= R:
                    m = jnp.clip(n + d - R, 0, blocks - 1)
                    part = jnp.dot(
                        t2_ref[m * W + e - d + R], v_ref[n * W + d], preferred_element_type=jnp.float32
                    )
                    total = part if total is None else total + part
            total = total.astype(second_ref.dtype)
            for p in range(rows):
                for h in range(PER):
                    at = h * depth + e * TILES
                    second_ref[at : at + TILES, p * LANES : (p + 1) * LANES] = total[
                        p * TILES : (p + 1) * TILES, h * LANES : (h + 1) * LANES
                    ]
        chunk = 5 if rows % 5 == 0 else 1
        for c in range(rows // chunk):
            both = jnp.dot(
                o_ref[n],
                second_ref[:, c * chunk * LANES : (c + 1) * chunk * LANES],
                preferred_element_type=jnp.float32,
            )
            for i in range(chunk):
                p = c * chunk + i
                at = slice(i * LANES, (i + 1) * LANES)
                x_ref[p * (depth + 1) : p * (depth + 1) + depth, :] = jnp.where(
                    lane < BS, both[:depth, at], both[depth:, at]
                )
        def rows_of(i, reach):
            return x_ref[pl.ds(i, reach, stride=depth + 1), :]

        pack_block(n, count_ref, select_ref, rows, rows_of, a_ref, c_ref)
        for d in range(W):
            first = offset_ref[n * W + d]

            def unit(u):
                load = packed_load(n, d, u, tiles, count_ref, c_ref)
                write_unit(out_ref, first + u, rows, load)

            units_loop(0, offset_ref[n * W + d + 1] - first, unit)
        return carry

    lax.fori_loop(0, blocks, block, 0)
    total = offset_ref[blocks * W]
    clear_units(out_ref, total, jnp.maximum(total + spare, base_units), rows)


def x_layout(three_center, offsets, counts, keep, limits, green, select, units, base_units, spare):
    rows, blocks = three_center.shape[:2]
    _, pieces = unit_shape(rows)
    depth = W * TILES
    reach = rows // SUB * SUB + SUB
    return pl.pallas_call(
        functools.partial(x_kernel, base_units, spare),
        in_specs=[pl.BlockSpec(memory_space=pltpu.SMEM)] * 4
        + [pl.BlockSpec(memory_space=pltpu.VMEM)] * 3,
        out_specs=pl.BlockSpec(memory_space=pltpu.VMEM),
        out_shape=jax.ShapeDtypeStruct((units * pieces, SUB, LANES), jnp.bfloat16),
        scratch_shapes=[
            pltpu.VMEM((TILES * blocks, LANES), jnp.float32),
            pltpu.VMEM((blocks * W, rows * TILES, LANES), jnp.bfloat16),
            pltpu.VMEM((PER * depth, rows * LANES), jnp.bfloat16),
            pltpu.VMEM((reach * (depth + 1), LANES), jnp.float32),
            pltpu.VMEM((blocks * W * BS, LANES), jnp.bfloat16),
            pltpu.VMEM((blocks * W // PER * BS, LANES), jnp.bfloat16),
            pltpu.VMEM((blocks * W, LANES, PER * LANES), jnp.bfloat16),
            pltpu.VMEM((blocks, PER * depth, PER * depth), jnp.bfloat16),
            pltpu.VMEM((W * BS // GROUP * reach, GROUP * BS), jnp.bfloat16),
            pltpu.VMEM((GROUP // PER, W * BS // GROUP * reach, LANES), jnp.float32),
        ],
        compiler_params=pltpu.CompilerParams(vmem_limit_bytes=56 << 20),
        cost_estimate=pl.CostEstimate(
            flops=blocks * rows * (7 * TILES * LANES * LANES * 4 + 16 * TILES * TILES * 9 * LANES),
            bytes_accessed=three_center.size * 8,
            transcendentals=0,
        ),
    )(offsets, counts, keep, limits, three_center.transpose(0, 2, 1, 3), green, select)


def more_units(total, t):
    turn = t % PARTS
    return t // PARTS * total + sum((total + r) // PARTS * (turn > r) for r in range(PARTS)), (total + turn) // PARTS


def exchange_kernel(base, total, most, pieces, more_ref, x_ref, keep_ref, out_ref, send_sem, recv_sem, own_sem):
    n_aux, n_orb = lax.axis_size("aux"), lax.axis_size("orb")
    targets = n_aux * n_orb
    aux, orb = lax.axis_index("aux"), lax.axis_index("orb")
    me = aux * n_orb + orb
    few, step = total // PARTS, PARTS - total % PARTS

    def spans(t, source, more):
        yield keep_ref, out_ref.at[source, pl.ds((2 * most + base) * pieces, keep_ref.shape[0])]
        size = base * pieces
        yield x_ref.at[pl.ds(t * size, size)], out_ref.at[source, pl.ds(most * pieces, size)]
        if more:
            size = more * pieces
            at, _ = more_units(total, t)
            yield (
                x_ref.at[pl.ds((targets * base + at) * pieces, size)],
                out_ref.at[source, pl.ds((most + base) * pieces, size)],
            )
            yield more_ref.at[pl.ds(at * pieces, size)], out_ref.at[source, pl.ds(0, size)]

    def by_size(t, act):
        if step == PARTS:
            act(few)
        else:
            pl.when(t % PARTS < step)(functools.partial(act, few))
            pl.when(t % PARTS >= step)(functools.partial(act, few + 1))

    def partner(i):
        turn = i // n_aux
        away = (turn + 1) // 2 * (1 - 2 * lax.rem(turn, 2)) + n_orb // 2
        return lax.rem(aux + lax.rem(i, n_aux), n_aux), lax.rem(orb + away + n_orb, n_orb)

    def copies(t, source, to, more):
        return [
            pltpu.make_async_remote_copy(
                src_ref=src,
                dst_ref=dst,
                send_sem=send_sem.at[k, t],
                recv_sem=recv_sem.at[k, source],
                device_id=to,
                device_id_type=pl.DeviceIdType.MESH,
            )
            for k, (src, dst) in enumerate(spans(t, source, more))
        ]

    def start(i, carry):
        to = partner(i)
        t = to[0] * n_orb + to[1]

        def act(more):
            for copy in copies(t, me, to, more):
                copy.start()

        pl.when(t != me)(lambda: by_size(t, act))
        return carry

    lax.fori_loop(0, targets, start, 0)

    def own(finish, more):
        for k, (src, dst) in enumerate(spans(me, me, more)):
            copy = pltpu.make_async_copy(src, dst, own_sem.at[k])
            copy.wait() if finish else copy.start()

    by_size(me, functools.partial(own, False))

    def finish(i, carry):
        to = partner(i)
        t = to[0] * n_orb + to[1]

        def received(more):
            for copy in copies(me, t, to, more):
                copy.wait_recv()

        def sent(more):
            for copy in copies(t, me, to, more):
                copy.wait_send()

        def both():
            by_size(me, received)
            by_size(t, sent)

        pl.when(t != me)(both)
        return carry

    lax.fori_loop(0, targets, finish, 0)
    by_size(me, functools.partial(own, True))


def exchange(base, most, pieces, total, outgoing, x, keep):
    targets = lax.axis_size("aux") * lax.axis_size("orb")
    return pl.pallas_call(
        functools.partial(exchange_kernel, base, total, most, pieces),
        in_specs=[pl.BlockSpec(memory_space=pl.ANY)] * 3,
        out_specs=pl.BlockSpec(memory_space=pl.ANY),
        out_shape=jax.ShapeDtypeStruct(
            (targets, (2 * most + base) * pieces + keep.shape[0], SUB, LANES), jnp.bfloat16
        ),
        scratch_shapes=[
            pltpu.SemaphoreType.DMA((4, targets)),
            pltpu.SemaphoreType.DMA((4, targets)),
            pltpu.SemaphoreType.DMA((4,)),
        ],
        compiler_params=pltpu.CompilerParams(has_side_effects=True),
    )(outgoing, x, keep)


def chi_kernel(rows, share_ref, left_ref, both_ref, held_ref, out_ref, l_ref, r_ref, k_ref):
    sources = left_ref.shape[0]
    tiles, pieces = unit_shape(rows)
    base = left_ref.shape[1] // pieces
    most = (both_ref.shape[1] // pieces - base) // 2
    whole, rest = rows // SUB, rows % SUB
    main = sources * whole * SUB

    def assemble(from_ref, first, to_ref, u, tiles=tiles):
        for j in range(tiles):
            at = slice((u * tiles + j) * LANES, (u * tiles + j + 1) * LANES)
            for s in range(sources):
                if whole:
                    i = first + j * whole
                    to_ref[s * whole * SUB : (s + 1) * whole * SUB, at] = jnp.concatenate(
                        [from_ref[s, i + q] for q in range(whole)], axis=0
                    )
            if rest:
                i = first + tiles * whole
                step = SUB // rest
                for s in range(0, sources, step):
                    to_ref[main + s * rest : main + (s + step) * rest, at] = jnp.concatenate(
                        [from_ref[s + t, i, j * rest : (j + 1) * rest, :] for t in range(step)],
                        axis=0,
                    )

    assemble(both_ref, (2 * most + base) * pieces, k_ref, 0, 1)
    keep = jnp.dot(k_ref[...], held_ref[...], preferred_element_type=jnp.float32)
    keep = keep.astype(l_ref.dtype)

    def fill(u):
        if u < base:
            assemble(left_ref, u * pieces, l_ref, u)
        else:
            assemble(both_ref, (u - base) * pieces, l_ref, u)
        assemble(both_ref, (most + u) * pieces, r_ref, u)
        for i in range(u * tiles, (u + 1) * tiles):
            at = slice(i * LANES, (i + 1) * LANES)
            l_ref[:, at] = l_ref[:, at] * keep[:, i : i + 1]

    def clear(u):
        at = slice(u * tiles * LANES, (u + 1) * tiles * LANES)
        l_ref[:, at] = jnp.zeros((l_ref.shape[0], tiles * LANES), l_ref.dtype)
        r_ref[:, at] = jnp.zeros((r_ref.shape[0], tiles * LANES), r_ref.dtype)

    for u in range(base + most):
        if u < base:
            fill(u)
        else:
            pl.when(u < share_ref[0])(functools.partial(fill, u))
            pl.when(u >= share_ref[0])(functools.partial(clear, u))
    chi = lax.dot_general(
        l_ref[...], r_ref[...], (((1,), (1,)), ((), ())), preferred_element_type=jnp.float32
    ).astype(out_ref.dtype)
    groups, height = out_ref.shape[:2]
    top = main // groups
    for a in range(groups):
        out_ref[a, :top, :] = chi[a * top : (a + 1) * top]
        if rest:
            low = height - top
            out_ref[a, top:, :] = chi[main + a * low : main + (a + 1) * low]


def chi_part(share, left, both, held, rows, groups):
    sources = left.shape[0]
    tiles, pieces = unit_shape(rows)
    functions = sources * rows
    units = (left.shape[1] // pieces + both.shape[1] // pieces) // 2
    depth = units * tiles * LANES
    return pl.pallas_call(
        functools.partial(chi_kernel, rows),
        in_specs=[pl.BlockSpec(memory_space=pltpu.SMEM)]
        + [pl.BlockSpec(memory_space=pltpu.VMEM)] * 3,
        out_specs=pl.BlockSpec(memory_space=pltpu.VMEM),
        out_shape=jax.ShapeDtypeStruct((groups, functions // groups, functions), jnp.float32),
        scratch_shapes=[pltpu.VMEM((functions, k), jnp.bfloat16) for k in (depth, depth, LANES)],
        compiler_params=pltpu.CompilerParams(vmem_limit_bytes=36 << 20),
    )(share, left, both, held)


def total_kernel(rows, cores, chunks, part_ref, out_ref, pair_ref, left_ref, near_ref, held_ref, right_ref, far_ref, *sems):
    n_aux, n_orb = lax.axis_size("aux"), lax.axis_size("orb")
    aux, orb = lax.axis_index("aux"), lax.axis_index("orb")
    chips = n_aux // cores
    chip, core = aux // cores, lax.rem(aux, cores)
    other = cores - 1 - core
    whole, rest = rows // SUB * SUB, rows % SUB
    pair_send, pair_recv, near_send, near_recv, far_send, far_recv = sems

    def remote(src, dst, send, recv, to):
        return pltpu.make_async_remote_copy(
            src_ref=src, dst_ref=dst, send_sem=send, recv_sem=recv,
            device_id=to, device_id_type=pl.DeviceIdType.MESH,
        )

    def pair(c, i):
        to = lax.rem(chip + i, chips)
        at = chunks[c]
        return remote(
            part_ref.at[to * cores + other, :, at], pair_ref.at[to, :, at],
            pair_send.at[c, i], pair_recv.at[c, i], (chip * cores + other, orb),
        )

    def near(c, i):
        at = chunks[c]
        return remote(
            left_ref.at[i, :, at], near_ref.at[i, :, at],
            near_send.at[c, i], near_recv.at[c, i], (lax.rem(chip + i, chips) * cores + core, orb),
        )

    def far(c, i):
        to = lax.rem(orb + i, n_orb)
        at = chunks[c]
        return remote(
            right_ref.at[to, :, at], far_ref.at[i, :, at], far_send.at[c, i], far_recv.at[c, i], (aux, to)
        )

    order = list(range(1, chips)) + [0]
    for c in range(len(chunks)):
        for i in order:
            pair(c, i).start()
    for c, at in enumerate(chunks):
        for i in order:
            to = lax.rem(chip + i, chips)
            pair(c, i).wait_recv()
            both = part_ref[to * cores + core, :, at] + pair_ref[to, :, at]
            if i:
                left_ref[i, :, at] = both.astype(left_ref.dtype)
                near(c, i).start()
            else:
                held_ref[:, at] = both
    for c, at in enumerate(chunks):
        total = held_ref[:, at]
        for i in range(1, chips):
            near(c, i).wait_recv()
            total = total + near_ref[i, :, at].astype(jnp.float32)
        held_ref[:, at] = total
        for o in range(n_orb):
            right_ref[o, :whole, at] = total[o * whole : (o + 1) * whole].astype(right_ref.dtype)
            if rest:
                low = n_orb * whole + o * rest
                tail = total[low // SUB * SUB : low // SUB * SUB + SUB]
                if low % SUB:
                    tail = pltpu.roll(tail, SUB - low % SUB, 0)
                right_ref[o, whole:, at] = tail.astype(right_ref.dtype)
        for i in range(1, n_orb):
            far(c, i).start()
    for c, at in enumerate(chunks):
        total = right_ref[orb, :, at].astype(jnp.float32)
        for i in range(1, n_orb):
            far(c, i).wait_recv()
            total = total + far_ref[i, :, at].astype(jnp.float32)
        out_ref[:, at] = total
    for c in range(len(chunks)):
        for i in range(chips):
            pair(c, i).wait_send()
        for i in range(1, chips):
            near(c, i).wait_send()
        for i in range(1, n_orb):
            far(c, i).wait_send()


def total_part(part, rows):
    n_aux, height, functions = part.shape
    n_orb = lax.axis_size("orb")
    cores = 2
    chips = n_aux // cores
    tall = -(-rows // SUB) * SUB
    cut = functions // LANES // 2 * LANES
    chunks = (slice(0, cut), slice(cut, functions))
    wide = jnp.float32
    return pl.pallas_call(
        functools.partial(total_kernel, rows, cores, chunks),
        in_specs=[pl.BlockSpec(memory_space=pltpu.VMEM)],
        out_specs=pl.BlockSpec(memory_space=pltpu.VMEM),
        out_shape=jax.ShapeDtypeStruct((tall, functions), wide),
        scratch_shapes=[
            pltpu.VMEM((chips, height, functions), wide),
            pltpu.VMEM((chips, height, functions), jnp.bfloat16),
            pltpu.VMEM((chips, height, functions), jnp.bfloat16),
            pltpu.VMEM((height, functions), wide),
            pltpu.VMEM((n_orb, tall, functions), jnp.bfloat16),
            pltpu.VMEM((n_orb, tall, functions), jnp.bfloat16),
        ]
        + [pltpu.SemaphoreType.DMA((2, k)) for k in (chips, chips, chips, chips, n_orb, n_orb)],
        compiler_params=pltpu.CompilerParams(has_side_effects=True, vmem_limit_bytes=36 << 20),
    )(part)


def body(three_center, atom_size, tensor_pattern, green_occ, green_virt, green_pattern):
    both = ("aux", "orb")
    n_aux, n_orb = lax.axis_size("aux"), lax.axis_size("orb")
    aux, orb = lax.axis_index("aux"), lax.axis_index("orb")
    rows, blocks = three_center.shape[0], three_center.shape[1]
    local_blocks = green_occ.shape[0]
    area = BS * BS
    targets = n_aux * n_orb
    functions = targets * rows
    tiles, pieces = unit_shape(rows)

    owned = jnp.arange(blocks, dtype=jnp.int32)[:, None]
    partner = owned + jnp.arange(W, dtype=jnp.int32)[None, :] - R
    inside = (partner >= 0) & (partner < blocks)
    catalog = jnp.arange(blocks, dtype=jnp.int32)
    partner_size = jnp.sum(jnp.where(partner[:, :, None] == catalog, atom_size, 0), axis=2)
    counts = jnp.clip(-(-atom_size // SUB) * SUB, BS // 2, BS)
    taken = -(-partner_size * counts[:, None] // (tiles * LANES)) * inside
    select = selections()
    before = jnp.arange(blocks * W + 1, dtype=jnp.int32)[:, None]
    before = before > jnp.arange(blocks * W, dtype=jnp.int32)[None, :]
    offsets = jnp.sum(jnp.where(before, taken.reshape(1, -1), 0), axis=1).astype(jnp.int32)
    largest = -(-(blocks * W - 2 * R) * TILES // (tiles * targets))
    base = -(-largest // 2)
    most = largest - base
    total = jnp.clip(-(-offsets[-1] * PARTS // targets) - base * PARTS, 0, most * PARTS)
    me = aux * n_orb + orb
    ahead, more = more_units(total, me)

    groups = tensor_pattern.shape[0]
    flags = [tensor_pattern.transpose(1, 2, 0).reshape(local_blocks * W, groups)]
    flags.append(green_pattern.reshape(local_blocks * W, 1))
    flags = (jnp.concatenate(flags, axis=1) > 0).astype(jnp.bfloat16)
    own = local_blocks * W
    flags = jnp.pad(flags, ((0, 0), (0, LANES - groups - 1))).reshape(-1)
    lines = -(-own * LANES // (BS * BS))
    flags = jnp.pad(flags, (0, lines * BS * BS - own * LANES)).reshape(lines, BS * BS)
    packed = [green_occ.reshape(own, BS * BS), green_virt.reshape(own, BS * BS), flags]
    packed = gather(jnp.concatenate(packed, axis=0), "orb")

    first, outgoing = send_layout(three_center, offsets, counts, select, base * targets, most * targets, targets // PARTS)
    packed, _ = lax.optimization_barrier((packed, first))
    left = lax.all_to_all(
        first.reshape(targets, base * pieces, SUB, LANES), both, split_axis=0, concat_axis=0, tiled=True
    )

    flags = packed[:, 2 * own :].reshape(n_orb, -1)[:, : own * LANES].reshape(blocks * W, LANES)
    green = jnp.concatenate(
        [packed[:, i * own : (i + 1) * own].reshape(n_orb, own * BS, BS) for i in range(2)], axis=2
    )
    mine = (orb * rows + jnp.arange(pieces * SUB, dtype=jnp.int32)) // ABS
    wanted = mine[:, None] == jnp.arange(LANES, dtype=jnp.int32)[None, :]
    keep = lax.dot_general(
        wanted.astype(flags.dtype),
        jnp.pad(flags, ((0, LANES - blocks * W), (0, 0))),
        (((1,), (1,)), ((), ())),
        preferred_element_type=jnp.float32,
    )
    held_pieces = rows // SUB + (1 if rows % SUB else 0)
    kept = keep[: held_pieces * SUB].astype(jnp.bfloat16).reshape(held_pieces, SUB, LANES)

    diagonal = jnp.arange(W, dtype=jnp.int32) == R
    green_all = flags[:, groups].reshape(blocks, W)
    green_keep = ((green_all > 0) | diagonal[None, :]) & inside
    limits = jnp.stack(
        [jnp.where(green_keep, partner_size, 0), jnp.broadcast_to(atom_size[:, None], (blocks, W))], axis=2
    )
    x = x_layout(
        three_center, offsets, counts, keep[:rows, : blocks * W], limits.reshape(-1), green, select,
        largest * targets, base * targets, targets // PARTS,
    )

    slot = jnp.arange(largest * tiles, dtype=jnp.int32) // tiles
    mine = jnp.where(slot < base, me * base + slot, targets * base + ahead + slot - base)[None, :]
    ends = jnp.pad(offsets[1:], (0, LANES - blocks * W))[:, None]
    held = (mine >= jnp.pad(offsets[:-1], (0, LANES - blocks * W))[:, None]) & (mine < ends)

    received = lax.switch(
        total,
        [functools.partial(exchange, base, most, pieces, k) for k in range(most * PARTS + 1)],
        outgoing,
        x,
        kept,
    )
    held = held.astype(jnp.bfloat16)
    part = chi_part((base + more).reshape(1), left, received, held, rows, n_aux)
    whole = rows // SUB * SUB
    chi = total_part(part, rows)[:rows]
    chi = jnp.concatenate(
        [
            chi[:, : targets * whole].reshape(rows, targets, whole),
            chi[:, targets * whole :].reshape(rows, targets, rows - whole),
        ],
        axis=2,
    )
    return chi.reshape(rows, functions)


def solution(mesh):
    return jax.shard_map(
        body,
        mesh=mesh,
        in_specs=(
            P(("aux", "orb"), None, None, None),
            P(),
            P("aux", "orb", None),
            P("orb", None, None),
            P("orb", None, None),
            P("orb", None),
        ),
        out_specs=P(("aux", "orb"), None),
        check_vma=False,
    )
```
